512 devices in a mesh: shot: 4 (over x), gx: 16 (over z_hi, y), gy: 8 (over z_lo, core).
Axes of the slice: x: 4, y: 4, z: 16 (z_hi: 4, z_lo: 4; z = z_hi * 4 + z_lo), core: 2. Of those that a mesh axis runs over, the one named last changes fastest.
Arguments:
- forward_now: float32 [4, 512, 256, 128], P('shot', 'gx', 'gy'), may hold values from -3 to 3
- forward_later: float32 [4, 512, 256, 128], P('shot', 'gx', 'gy'), may hold values from -3 to 3
- adjoint_now: float32 [4, 512, 256, 128], P('shot', 'gx', 'gy'), may hold values from -3 to 3
- adjoint_later: float32 [4, 512, 256, 128], P('shot', 'gx', 'gy'), may hold values from -3 to 3
- courant: float32 [512, 256, 128], P('gx', 'gy'), may hold values from 0.15 to 0.45
- source_cells: int32 [4, 16, 3], P('shot'), may hold values from 0 to 511, as said below
- source_wave: float32 [4, 3, 16], P('shot'), may hold values from -6 to 6
- receiver_cells: int32 [4, 4096, 3], P('shot'), may hold values from 0 to 511, as said below
- residual: float32 [4, 3, 4096], P('shot'), may hold values from -6 to 6
Outputs:
- forward_first: float32 [4, 512, 256, 128], P('shot', 'gx', 'gy')
- adjoint_first: float32 [4, 512, 256, 128], P('shot', 'gx', 'gy')
- gradient: float32 [512, 256, 128], P('gx', 'gy')
The draws below stay inside these ranges and needn't reach their ends.
Inputs may be any that keep to these rules, and one draw needn't show every extreme that they name: `source_cells`: entry [s, i] holds the first, second and depth cell index of source i of shot group s, each inside the grid of 512 x 256 x 128 cells; cells may repeat. `receiver_cells`: entry [s, r] holds the first, second and depth cell index of receiver r of shot group s, each inside the grid of 512 x 256 x 128 cells; cells may repeat.
All inputs are finite; a program needn't handle non-finite values.
Results may differ from the reference program's by a relative error of at most 0.0003.
Values sent between devices are 32-bit elements; how exact they have to be, the bound alone decides.
A program may use at most 64 MiB of HBM per device.

```python
import math
import jax
import jax.numpy as jnp
from jax import lax

NZ = 128
STEPS = 3
NSRC = 16
NREC = 4096
SHOTS = 4
NX = 512
NY = 256


def draw_cells(key, count):
    upper = jnp.array([NX, NY, NZ], jnp.int32)
    cells = jax.random.randint(key, (SHOTS, count, 3), 0, upper)
    cells = cells.at[0, 0, 0].set(NX - 1)
    cells = cells.at[0, 1, 0].set(0)
    return cells.astype(jnp.int32)


def draw_source_cells(key, part):
    return draw_cells(jax.random.fold_in(key, 11), NSRC)


def draw_receiver_cells(key, part):
    return draw_cells(jax.random.fold_in(key, 23), NREC)


def plane_waves(key, later):
    keys = jax.random.split(key, 7)
    magnitude = jax.random.randint(keys[0], (SHOTS, 6), 5, 11)
    flipped = 2 * jax.random.randint(keys[1], (SHOTS, 6), 0, 2) - 1
    along_x = magnitude * flipped
    along_y = jax.random.randint(keys[2], (SHOTS, 6), -8, 9)
    along_z = jax.random.randint(keys[3], (SHOTS, 6), -8, 9)
    offsets = jax.random.randint(keys[4], (SHOTS, 6), 0, 128)
    delays = jax.random.randint(keys[5], (SHOTS, 6), 2, 7)
    weights = jax.random.uniform(keys[6], (SHOTS, 6), jnp.float32, 0.15, 0.4)
    starts = offsets + 128 - later * delays
    cells_x = jnp.arange(NX, dtype=jnp.int32)[None, :, None, None]
    cells_y = jnp.arange(NY, dtype=jnp.int32)[None, None, :, None]
    cells_z = jnp.arange(NZ, dtype=jnp.int32)[None, None, None, :]
    total = jnp.zeros((SHOTS, NX, NY, NZ), jnp.float32)
    for wave in range(6):
        phases = along_x[:, wave, None, None, None] * cells_x + along_y[:, wave, None, None, None] * cells_y
        phases = phases + along_z[:, wave, None, None, None] * cells_z + starts[:, wave, None, None, None]
        phases = jnp.mod(phases + 4096, 128)
        total = total + weights[:, wave, None, None, None] * jnp.cos(phases.astype(jnp.float32) * (2.0 * math.pi / 128.0))
    return total


def band_field(key, later, salt):
    base = jax.random.fold_in(key, salt)
    smooth = plane_waves(base, later)
    noise_key = jax.random.fold_in(base, 100 + later)
    shape = (SHOTS, NX, NY, NZ)
    noise = jnp.clip(0.02 * jax.random.normal(noise_key, shape, jnp.float32), -0.1, 0.1)
    return (smooth + noise).astype(jnp.float32)


def draw_forward_now(key, part):
    return band_field(key, 0, 31)


def draw_forward_later(key, part):
    return band_field(key, 1, 31)


def draw_adjoint_now(key, part):
    return band_field(key, 0, 47)


def draw_adjoint_later(key, part):
    return band_field(key, 1, 47)


def block_levels(own_key, shape, cuts, least, high):
    loudness = 1.0
    for position, parts in cuts:
        draws = jax.random.uniform(jax.random.fold_in(jax.random.fold_in(own_key, 6), position), (parts,), jnp.float32, least / len(cuts), high / len(cuts))
        loudness = loudness * jnp.repeat(jnp.exp(draws), shape[position] // parts).reshape((-1,) + (1,) * (len(shape) - 1 - position))
    return loudness


def centred(stream_key, extent, deviation, most, cuts=(), kind=jnp.bfloat16):
    entries = jax.random.normal(stream_key, extent, jnp.float32) * deviation
    if len(cuts) > 0:
        entries = block_levels(stream_key, extent, cuts, -0.22, 0.18) * entries
    return jnp.clip(entries, min=-most, max=most).astype(kind)


def setup_inputs(seed: int = 0) -> dict:
    arg_keys = jax.random.split(jax.random.key(seed), 10)
    return {
        "forward_now": draw_forward_now(jax.random.fold_in(arg_keys[9], 71), 0),
        "forward_later": draw_forward_later(jax.random.fold_in(arg_keys[9], 71), 0),
        "adjoint_now": draw_adjoint_now(jax.random.fold_in(arg_keys[9], 71), 0),
        "adjoint_later": draw_adjoint_later(jax.random.fold_in(arg_keys[9], 71), 0),
        "courant": jnp.clip(0.15 + 0.29999998 * jax.random.uniform(arg_keys[4], (NX, NY, NZ), jnp.float32) ** block_levels(arg_keys[4], (NX, NY, NZ), ((0, 16), (1, 8)), -0.2, 0.2), 0.15, 0.45),
        "source_cells": draw_source_cells(jax.random.fold_in(arg_keys[9], 71), 0),
        "source_wave": centred(arg_keys[6], (SHOTS, STEPS, NSRC), 1.0, 6.0, ((0, 4),), jnp.float32),
        "receiver_cells": draw_receiver_cells(jax.random.fold_in(arg_keys[9], 71), 0),
        "residual": centred(arg_keys[8], (SHOTS, STEPS, NREC), 1.0, 6.0, ((0, 4),), jnp.float32),
    }


COEFFS = (-205.0 / 72.0, 8.0 / 5.0, -1.0 / 5.0, 8.0 / 315.0, -1.0 / 560.0)
GRAD_SCALE = 0.1


def stencil(extended):
    full = jnp.pad(extended, [(0, 0)] * (extended.ndim - 1) + [(4, 4)])
    rows_x = extended.shape[-3] - 8
    rows_y = extended.shape[-2] - 8
    depth = extended.shape[-1]

    def shifted(step_x, step_y, step_z):
        return full[..., 4 + step_x:4 + step_x + rows_x, 4 + step_y:4 + step_y + rows_y, 4 + step_z:4 + step_z + depth]

    summed = (3.0 * COEFFS[0]) * shifted(0, 0, 0)
    for reach in range(1, 5):
        pairs = (shifted(reach, 0, 0) + shifted(-reach, 0, 0)) + (shifted(0, reach, 0) + shifted(0, -reach, 0))
        pairs = pairs + (shifted(0, 0, reach) + shifted(0, 0, -reach))
        summed = summed + COEFFS[reach] * pairs
    return summed


def pad_sides(field):
    return jnp.pad(field, ((4, 4), (4, 4), (0, 0)))


def reference(forward_now, forward_later, adjoint_now, adjoint_later, courant, source_cells, source_wave, receiver_cells, residual):
    squared = courant * courant

    def one_group(items):
        wave_now, wave_later, dual_now, dual_later, sources, amplitude, receivers, misfit = items
        summed = jnp.zeros(courant.shape, jnp.float32)
        for step in range(STEPS):
            curved_wave = stencil(pad_sides(wave_now))
            curved_dual = stencil(pad_sides(dual_now))
            summed = summed + 2.0 * courant * dual_now * curved_wave
            wave_early = 2.0 * wave_now - wave_later + squared * curved_wave
            wave_early = wave_early.at[sources[:, 0], sources[:, 1], sources[:, 2]].add(amplitude[step])
            dual_early = 2.0 * dual_now - dual_later + squared * curved_dual
            dual_early = dual_early.at[receivers[:, 0], receivers[:, 1], receivers[:, 2]].add(misfit[step])
            wave_later, wave_now = wave_now, wave_early
            dual_later, dual_now = dual_now, dual_early
        return wave_now, dual_now, summed

    forward_first, adjoint_first, terms = lax.map(one_group, (forward_now, forward_later, adjoint_now, adjoint_later, source_cells, source_wave, receiver_cells, residual))
    return forward_first, adjoint_first, GRAD_SCALE * jnp.sum(terms, axis=0)
```

```python
import functools

import jax
import jax.numpy as jnp
from jax import lax
from jax.experimental import pallas as pl
from jax.experimental.pallas import tpu as pltpu
from jax.sharding import PartitionSpec as P

STEPS = 3
W = 4
PADY = 8
SLOTS = 256
LANES = 128
COEFFS = (-205.0 / 72.0, 8.0 / 5.0, -1.0 / 5.0, 8.0 / 315.0, -1.0 / 560.0)
GRAD_SCALE = 0.1
MESH = pl.DeviceIdType.MESH
VMEM_LIMIT = 48 * 1024 * 1024


def scatter_kernel(rows_x, rows_y, chunks, feats_ref, mask_ref, sfeats_ref, out_p, out_q, rank_ref):
    cells = rows_x * rows_y
    f32, bf16 = jnp.float32, jnp.bfloat16
    nt = (((1,), (1,)), ((), ()))

    def spread(by_row, by_col, out, add):
        slots = by_row.shape[1]
        place = by_row[0:1, :] * float(rows_y) + by_row[1:2, :]
        ids = lax.broadcasted_iota(jnp.int32, (cells, slots), 0).astype(f32)
        left = (ids == place).astype(f32).astype(bf16)
        lane = lax.broadcasted_iota(jnp.int32, (slots, LANES), 1).astype(f32)
        hit = lane == by_col[:, 2:3]
        for step in range(STEPS):
            high = jnp.where(hit, by_col[:, 3 + step : 4 + step], 0.0)
            low = jnp.where(hit, by_col[:, 6 + step : 7 + step], 0.0)
            right = jnp.concatenate([high, low], axis=1).astype(bf16)
            both = jnp.dot(left, right, preferred_element_type=f32)
            total = (both[:, :LANES] + both[:, LANES:]).reshape(rows_x, rows_y, LANES)
            if add:
                out[step] = out[step] + total
            else:
                out[step] = total

    sfeats = sfeats_ref[...]
    inside = (
        (sfeats[0:1] >= 0.0)
        & (sfeats[0:1] < float(rows_x))
        & (sfeats[1:2] >= 0.0)
        & (sfeats[1:2] < float(rows_y))
    )
    sfeats = jnp.where(inside, sfeats, 0.0)
    spread(sfeats, sfeats.T, out_p, False)

    mask = mask_ref[...]
    ones = mask.astype(bf16)
    row = lax.broadcasted_iota(jnp.int32, (LANES, LANES), 0)
    col = lax.broadcasted_iota(jnp.int32, (LANES, LANES), 1)
    upper = (row <= col).astype(f32).astype(bf16)
    inclusive = jnp.dot(ones, upper, preferred_element_type=f32)
    totals = jnp.broadcast_to(inclusive[:, LANES - 1 : LANES], (chunks, LANES)).astype(bf16)
    crow = lax.broadcasted_iota(jnp.int32, (chunks, chunks), 0)
    ccol = lax.broadcasted_iota(jnp.int32, (chunks, chunks), 1)
    before = (ccol < crow).astype(f32).astype(bf16)
    offsets = jnp.dot(before, totals, preferred_element_type=f32)
    rank_ref[...] = jnp.where(mask > 0.5, offsets + inclusive - 1.0, -1.0)
    count = jnp.sum(mask).astype(jnp.int32)
    out_q[...] = jnp.zeros_like(out_q)

    def one_round(turn, carry):
        slot = lax.broadcasted_iota(jnp.int32, (SLOTS, LANES), 0).astype(f32)
        base = (turn * SLOTS).astype(f32)
        by_row = jnp.zeros((16, SLOTS), f32)
        by_col = jnp.zeros((SLOTS, 16), f32)
        for chunk in range(chunks):
            rank = rank_ref[chunk : chunk + 1, :] - base
            pick = (slot == rank).astype(f32).astype(bf16)
            part = feats_ref[:, chunk * LANES : (chunk + 1) * LANES].astype(bf16)
            by_row = by_row + lax.dot_general(part, pick, nt, preferred_element_type=f32)
            by_col = by_col + lax.dot_general(pick, part, nt, preferred_element_type=f32)
        spread(by_row, by_col, out_q, True)
        return carry

    lax.fori_loop(0, (count + SLOTS - 1) // SLOTS, one_round, 0)


def features(cells, values, start_x, start_y):
    count = cells.shape[0]
    high = lax.reduce_precision(values, 8, 7)
    local = cells.T - jnp.stack([start_x, start_y, jnp.int32(0)])[:, None]
    rows = [local.astype(jnp.float32), high, values - high, jnp.zeros((7, count), jnp.float32)]
    padded = -(-count // LANES) * LANES
    if padded == count:
        return jnp.concatenate(rows, 0)
    rows = jnp.concatenate(rows, 0)
    tail = jnp.full((16, padded - count), -1.0, jnp.float32)
    return jnp.concatenate([rows, tail], 1)


def wave_kernel(
    sizes, p0, p2, q0, q2, courant, add_p, add_q, out_p, out_q, out_g,
    ext, last, cour, adds, final, gacc, gout, rbuf, ysend, yrecv,
    load_sem, xs, xr, ys, yr, gs, gr, hs, hr, store_sem,
):
    n_shot, n_gx, n_gy, rx, ry = sizes
    me_s = lax.axis_index("shot")
    me_x = lax.axis_index("gx")
    me_y = lax.axis_index("gy")
    fields = (p0, q0)
    mid_x = pl.ds(W, rx)
    mid_y = pl.ds(PADY, ry)
    part = rx // n_shot

    loads = []

    def load(src, dst):
        copy = pltpu.make_async_copy(src, dst, load_sem.at[len(loads)])
        copy.start()
        loads.append(copy)

    load(p0, ext.at[0, 0, mid_x, mid_y])
    load(q0, ext.at[0, 1, mid_x, mid_y])
    load(courant, cour)
    load(p2, last.at[0])
    load(q2, last.at[1])
    load(add_p, adds.at[0])
    load(add_q, adds.at[1])

    for step in range(STEPS):
        for f in range(2):
            zx = jnp.zeros((W, ry, LANES), jnp.float32)
            zy = jnp.zeros((rx, W, LANES), jnp.float32)

            @pl.when(me_x == 0)
            def _():
                ext[step, f, 0:W, PADY : PADY + ry, :] = zx

            @pl.when(me_x == n_gx - 1)
            def _():
                ext[step, f, W + rx : 2 * W + rx, PADY : PADY + ry, :] = zx

            @pl.when(me_y == 0)
            def _():
                yrecv[step, f, 0] = zy

            @pl.when(me_y == n_gy - 1)
            def _():
                yrecv[step, f, 1] = zy

    barrier = pltpu.get_barrier_semaphore()
    has = (me_x < n_gx - 1, me_x > 0, me_y < n_gy - 1, me_y > 0)
    up_x = jnp.minimum(me_x + 1, n_gx - 1)
    down_x = jnp.maximum(me_x - 1, 0)
    up_y = jnp.minimum(me_y + 1, n_gy - 1)
    down_y = jnp.maximum(me_y - 1, 0)
    ids = ({"gx": up_x}, {"gx": down_x}, {"gy": up_y}, {"gy": down_y})
    for k in range(4):

        @pl.when(has[k])
        def _():
            pl.semaphore_signal(barrier, inc=1, device_id=ids[k], device_id_type=MESH)

    peers = [lax.rem(me_s + d, n_shot) for d in range(1, n_shot)]
    for peer in peers:
        pl.semaphore_signal(barrier, inc=1, device_id={"shot": peer}, device_id_type=MESH)
    expected = n_shot - 1
    for k in range(4):
        expected = expected + has[k].astype(jnp.int32)
    pl.semaphore_wait(barrier, expected)

    def x_copy(step, f, side):
        first = (rx - W) if side == 0 else 0
        if step == 0:
            src = fields[f].at[pl.ds(first, W)]
        else:
            src = ext.at[step, f, pl.ds(W + first, W), mid_y]
        dst = ext.at[step, f, pl.ds(0 if side == 0 else W + rx, W), mid_y]
        return pltpu.make_async_remote_copy(
            src_ref=src, dst_ref=dst, send_sem=xs.at[step, f, side], recv_sem=xr.at[step, f, side],
            device_id=ids[side], device_id_type=MESH,
        )

    def y_copy(step, f, side):
        return pltpu.make_async_remote_copy(
            src_ref=ysend.at[step, f, side], dst_ref=yrecv.at[step, f, side],
            send_sem=ys.at[step, f, side], recv_sem=yr.at[step, f, side],
            device_id=ids[2 + side], device_id_type=MESH,
        )

    def start_x(step, f):
        for side in range(2):

            @pl.when(has[side])
            def _():
                x_copy(step, f, side).start()

    def start_y(step, f):
        ysend[step, f, 0] = ext[step, f, W : W + rx, PADY + ry - W : PADY + ry, :]
        ysend[step, f, 1] = ext[step, f, W : W + rx, PADY : PADY + W, :]
        for side in range(2):

            @pl.when(has[2 + side])
            def _():
                y_copy(step, f, side).start()

    def wait_x(step, f):
        for side in range(2):

            @pl.when(has[1 - side])
            def _():
                x_copy(step, f, side).wait_recv()

    def wait_y(step, f):
        for side in range(2):

            @pl.when(has[3 - side])
            def _():
                y_copy(step, f, side).wait_recv()

        ext[step, f, W : W + rx, PADY - W : PADY, :] = yrecv[step, f, 0]
        ext[step, f, W : W + rx, PADY + ry : PADY + ry + W, :] = yrecv[step, f, 1]

    lane = lax.broadcasted_iota(jnp.int32, (ry, LANES), 1)

    def plane(step, f, x):
        here = ext[step, f, x + W, PADY : PADY + ry, :]
        total = (3.0 * COEFFS[0]) * here
        for k in range(1, W + 1):
            pairs = (
                ext[step, f, x + W + k, PADY : PADY + ry, :] + ext[step, f, x + W - k, PADY : PADY + ry, :]
            ) + (
                ext[step, f, x + W, PADY + k : PADY + ry + k, :]
                + ext[step, f, x + W, PADY - k : PADY + ry - k, :]
            )
            right = jnp.where(lane < LANES - k, pltpu.roll(here, LANES - k, 1), 0.0)
            left = jnp.where(lane >= k, pltpu.roll(here, k, 1), 0.0)
            total = total + COEFFS[k] * (pairs + (right + left))
        return here, total

    def previous(step, f, x):
        if step == 0:
            return last[f, x]
        return ext[step - 1, f, x + W, PADY : PADY + ry, :]

    def advance(step, f, x):
        here, curved = plane(step, f, x)
        if f == 0:
            term = ext[step, 1, x + W, PADY : PADY + ry, :] * curved
            gacc[x] = term if step == 0 else gacc[x] + term
        speed = cour[x]
        fresh = 2.0 * here - previous(step, f, x) + (speed * speed) * curved + adds[f, step, x]
        if step < STEPS - 1:
            ext[step + 1, f, x + W, PADY : PADY + ry, :] = fresh
        else:
            final[f, x] = fresh

    def planes(step, f, low, high):
        def body(x, carry):
            advance(step, f, x)
            return carry

        lax.fori_loop(low, high, body, 0)

    for f in range(2):
        start_x(0, f)
    loads[0].wait()
    start_y(0, 0)
    loads[1].wait()
    start_y(0, 1)
    for copy in loads[2:]:
        copy.wait()
    stores = []
    reduce_sends = []
    for step in range(STEPS):
        for f in range(2):
            wait_y(step, f)
            planes(step, f, W, rx - W)
        for f in range(2):
            wait_x(step, f)
            planes(step, f, 0, W)
            planes(step, f, rx - W, rx)
            if step < STEPS - 1:
                start_x(step + 1, f)
                start_y(step + 1, f)
            else:
                copy = pltpu.make_async_copy(final.at[f], (out_p, out_q)[f], store_sem.at[f])
                copy.start()
                stores.append(copy)
            if step == STEPS - 1 and f == 0:
                for d, peer in enumerate(peers):
                    copy = pltpu.make_async_remote_copy(
                        src_ref=gacc.at[pl.ds(peer * part, part)], dst_ref=rbuf.at[d],
                        send_sem=gs.at[d], recv_sem=gr.at[d],
                        device_id={"shot": peer}, device_id_type=MESH,
                    )
                    copy.start()
                    reduce_sends.append(copy)

    for copy in reduce_sends:
        copy.wait_recv()
    mine = pl.ds(me_s * part, part)
    total = gacc[mine]
    for d in range(n_shot - 1):
        total = total + rbuf[d]
    gout[mine] = total * ((2.0 * GRAD_SCALE) * cour[mine])
    gathers = []
    for d, peer in enumerate(peers):
        copy = pltpu.make_async_remote_copy(
            src_ref=gout.at[mine], dst_ref=gout.at[mine], send_sem=hs.at[d], recv_sem=hr.at[d],
            device_id={"shot": peer}, device_id_type=MESH,
        )
        copy.start()
        gathers.append(copy)
    for d, copy in enumerate(gathers):
        other = lax.rem(me_s + n_shot - 1 - d, n_shot)
        theirs = gout.at[pl.ds(other * part, part)]
        pltpu.make_async_remote_copy(
            src_ref=theirs, dst_ref=theirs, send_sem=hs.at[d], recv_sem=hr.at[d],
            device_id={"shot": other}, device_id_type=MESH,
        ).wait_recv()
    copy = pltpu.make_async_copy(gout, out_g, store_sem.at[2])
    copy.start()
    stores.append(copy)
    for step in range(STEPS):
        for f in range(2):
            for side in range(2):

                @pl.when(has[side])
                def _():
                    x_copy(step, f, side).wait_send()

                @pl.when(has[2 + side])
                def _():
                    y_copy(step, f, side).wait_send()

    for copy in reduce_sends + gathers:
        copy.wait_send()
    for copy in stores:
        copy.wait()


def shards(
    mesh_sizes, forward_now, forward_later, adjoint_now, adjoint_later, courant,
    source_cells, source_wave, receiver_cells, residual,
):
    rx, ry, depth = courant.shape
    n_shot, n_gx, n_gy = mesh_sizes
    f32 = jnp.float32
    start_x = (lax.axis_index("gx") * rx).astype(jnp.int32)
    start_y = (lax.axis_index("gy") * ry).astype(jnp.int32)
    feats = features(receiver_cells[0], residual[0], start_x, start_y)
    sfeats = features(source_cells[0], source_wave[0], start_x, start_y)
    mask = (feats[0] >= 0) & (feats[0] < rx) & (feats[1] >= 0) & (feats[1] < ry)
    chunks = feats.shape[1] // LANES
    mask = mask.astype(f32).reshape(chunks, LANES)
    whole = pl.BlockSpec(memory_space=pltpu.VMEM)
    anywhere = pl.BlockSpec(memory_space=pl.ANY)
    block = jax.ShapeDtypeStruct((rx, ry, depth), f32)
    added = jax.ShapeDtypeStruct((STEPS, rx, ry, depth), f32)
    add_p, add_q = pl.pallas_call(
        functools.partial(scatter_kernel, rx, ry, chunks),
        out_shape=(added, added),
        in_specs=[whole] * 3,
        out_specs=(whole, whole),
        scratch_shapes=[pltpu.VMEM((chunks, LANES), f32)],
        compiler_params=pltpu.CompilerParams(vmem_limit_bytes=VMEM_LIMIT),
        name="scatter",
    )(feats, mask, sfeats)
    sizes = (n_shot, n_gx, n_gy, rx, ry)
    dma = pltpu.SemaphoreType.DMA
    out_p, out_q, out_g = pl.pallas_call(
        functools.partial(wave_kernel, sizes),
        out_shape=(block, block, block),
        in_specs=[anywhere] * 7,
        out_specs=(anywhere,) * 3,
        scratch_shapes=[
            pltpu.VMEM((STEPS, 2, rx + 2 * W, ry + 2 * PADY, depth), f32),
            pltpu.VMEM((2, rx, ry, depth), f32),
            pltpu.VMEM((rx, ry, depth), f32),
            pltpu.VMEM((2, STEPS, rx, ry, depth), f32),
            pltpu.VMEM((2, rx, ry, depth), f32),
            pltpu.VMEM((rx, ry, depth), f32),
            pltpu.VMEM((rx, ry, depth), f32),
            pltpu.VMEM((n_shot - 1, rx // n_shot, ry, depth), f32),
            pltpu.VMEM((STEPS, 2, 2, rx, W, depth), f32),
            pltpu.VMEM((STEPS, 2, 2, rx, W, depth), f32),
            dma((7,)),
            dma((STEPS, 2, 2)),
            dma((STEPS, 2, 2)),
            dma((STEPS, 2, 2)),
            dma((STEPS, 2, 2)),
            dma((n_shot - 1,)),
            dma((n_shot - 1,)),
            dma((n_shot - 1,)),
            dma((n_shot - 1,)),
            dma((3,)),
        ],
        compiler_params=pltpu.CompilerParams(
            collective_id=0, has_side_effects=True, vmem_limit_bytes=VMEM_LIMIT
        ),
        name="window",
    )(
        forward_now[0], forward_later[0], adjoint_now[0], adjoint_later[0], courant, add_p, add_q,
    )
    return out_p[None], out_q[None], out_g


def solution(mesh):
    field = P("shot", "gx", "gy", None)
    listed = P("shot", None, None)
    sizes = (mesh.shape["shot"], mesh.shape["gx"], mesh.shape["gy"])
    return jax.shard_map(
        functools.partial(shards, sizes),
        mesh=mesh,
        in_specs=(field, field, field, field, P("gx", "gy", None), listed, listed, listed, listed),
        out_specs=(field, field, P("gx", "gy", None)),
        check_vma=False,
    )
```

```python
import functools

import jax
import jax.numpy as jnp
from jax import lax
from jax.experimental import pallas as pl
from jax.experimental.pallas import tpu as pltpu
from jax.sharding import PartitionSpec as P

STEPS = 3
W = 4
PADY = 8
SLOTS = 256
LANES = 128
COEFFS = (-205.0 / 72.0, 8.0 / 5.0, -1.0 / 5.0, 8.0 / 315.0, -1.0 / 560.0)
GRAD_SCALE = 0.1
MESH = pl.DeviceIdType.MESH
WINDOW_LIMIT = 64_000_000
RING = 4


def scatter_kernel(
    rows_x, rows_y, chunks, scells, swave, cells_ref, values_ref, out_p, out_q, rank_ref, feats_ref
):
    cells = rows_x * rows_y
    f32, bf16 = jnp.float32, jnp.bfloat16
    nt = (((1,), (1,)), ((), ()))
    base_x = lax.axis_index("gx") * rows_x
    base_y = lax.axis_index("gy") * rows_y
    out_p[...] = jnp.zeros_like(out_p)
    out_q[...] = jnp.zeros_like(out_q)

    depth_ids = lax.broadcasted_iota(jnp.int32, (1, LANES), 1)

    def one_source(i, carry):
        x = scells[i, 0] - base_x
        y = scells[i, 1] - base_y

        @pl.when((x >= 0) & (x < rows_x) & (y >= 0) & (y < rows_y))
        def _():
            for step in range(STEPS):
                line = out_p[step, x, pl.ds(y, 1), :]
                out_p[step, x, pl.ds(y, 1), :] = line + jnp.where(depth_ids == scells[i, 2], swave[step, i], 0.0)

        return carry

    lax.fori_loop(0, scells.shape[0], one_source, 0)

    x = (cells_ref[0:chunks, :] - base_x).astype(f32)
    y = (cells_ref[chunks : 2 * chunks, :] - base_y).astype(f32)
    inside = (x >= 0.0) & (x < float(rows_x)) & (y >= 0.0) & (y < float(rows_y))
    mask = jnp.where(inside, 1.0, 0.0)
    high = values_ref[...].astype(bf16).astype(f32)
    low = values_ref[...] - high
    parts = [x, y, cells_ref[2 * chunks : 3 * chunks, :].astype(f32)]
    parts += [high[s * chunks : (s + 1) * chunks] for s in range(STEPS)]
    parts += [low[s * chunks : (s + 1) * chunks] for s in range(STEPS)]
    feats_ref[...] = jnp.zeros_like(feats_ref)
    for i, values in enumerate(parts):
        for chunk in range(chunks):
            feats_ref[16 * chunk + i : 16 * chunk + i + 1, :] = values[chunk : chunk + 1, :]
    ones = mask.astype(bf16)
    row = lax.broadcasted_iota(jnp.int32, (LANES, LANES), 0)
    col = lax.broadcasted_iota(jnp.int32, (LANES, LANES), 1)
    upper = (row <= col).astype(f32).astype(bf16)
    inclusive = jnp.dot(ones, upper, preferred_element_type=f32)
    totals = jnp.broadcast_to(inclusive[:, LANES - 1 : LANES], (chunks, LANES)).astype(bf16)
    crow = lax.broadcasted_iota(jnp.int32, (chunks, chunks), 0)
    ccol = lax.broadcasted_iota(jnp.int32, (chunks, chunks), 1)
    before = (ccol < crow).astype(f32).astype(bf16)
    offsets = jnp.dot(before, totals, preferred_element_type=f32)
    rank_ref[...] = jnp.where(inside, offsets + inclusive - 1.0, -1.0)
    count = jnp.sum(mask).astype(jnp.int32)

    def one_round(turn, carry):
        slot = lax.broadcasted_iota(jnp.int32, (SLOTS, LANES), 0).astype(f32)
        base = (turn * SLOTS).astype(f32)
        by_row = jnp.zeros((16, SLOTS), f32)
        by_col = jnp.zeros((SLOTS, 16), f32)
        for chunk in range(chunks):
            rank = rank_ref[chunk : chunk + 1, :] - base
            pick = (slot == rank).astype(f32).astype(bf16)
            part = feats_ref[16 * chunk : 16 * chunk + 16, :].astype(bf16)
            by_row = by_row + lax.dot_general(part, pick, nt, preferred_element_type=f32)
            by_col = by_col + lax.dot_general(pick, part, nt, preferred_element_type=f32)
        place = by_row[0:1, :] * float(rows_y) + by_row[1:2, :]
        ids = lax.broadcasted_iota(jnp.int32, (cells, SLOTS), 0).astype(f32)
        left = (ids == place).astype(f32).astype(bf16)
        lane = lax.broadcasted_iota(jnp.int32, (SLOTS, LANES), 1).astype(f32)
        hit = lane == by_col[:, 2:3]
        for step in range(STEPS):
            upper_part = jnp.where(hit, by_col[:, 3 + step : 4 + step], 0.0)
            lower_part = jnp.where(hit, by_col[:, 6 + step : 7 + step], 0.0)
            right = jnp.concatenate([upper_part, lower_part], axis=1).astype(bf16)
            both = jnp.dot(left, right, preferred_element_type=f32)
            total = (both[:, :LANES] + both[:, LANES:]).reshape(rows_x, rows_y, LANES)
            out_q[step] = out_q[step] + total
        return carry

    lax.fori_loop(0, (count + SLOTS - 1) // SLOTS, one_round, 0)


def finish_kernel(a, b, c, out_a, out_b, out_c, buf, sems_in, sems_out):
    pairs = ((a, out_a), (b, out_b), (c, out_c))
    ins = [pltpu.make_async_copy(src, buf.at[i], sems_in.at[i]) for i, (src, _) in enumerate(pairs)]
    outs = [pltpu.make_async_copy(buf.at[i], dst, sems_out.at[i]) for i, (_, dst) in enumerate(pairs)]
    for copy in ins:
        copy.start()
    for copy_in, copy_out in zip(ins, outs):
        copy_in.wait()
        copy_out.start()
    for copy in outs:
        copy.wait()


def wave_kernel(
    sizes, p0, p2, q0, q2, courant, add_p, add_q, out_p, out_q, out_g,
    ext, last, cour, adds, final, gacc, gout, rbuf_a, rbuf_b, ysend, yrecv, relay,
    load_sem, xs, xr, ys, yr, gs, gr, hs, hr, ls, lr, store_sem,
):
    n_shot, n_gx, n_gy, rx, ry = sizes
    me_s = lax.axis_index("shot")
    me_x = lax.axis_index("gx")
    me_y = lax.axis_index("gy")
    fields = (p0, q0)
    mid_x = pl.ds(W, rx)
    mid_y = pl.ds(PADY, ry)
    ring = lax.rem(me_x, RING)
    group = me_x // RING
    groups = n_gx // RING

    loads = []

    def load(src, dst):
        copy = pltpu.make_async_copy(src, dst, load_sem.at[len(loads)])
        copy.start()
        loads.append(copy)

    load(p0, ext.at[0, 0, mid_x, mid_y])
    load(q0, ext.at[0, 1, mid_x, mid_y])
    load(courant, cour)
    load(p2, last.at[0])
    load(q2, last.at[1])
    load(add_p, adds.at[0])
    load(add_q, adds.at[1])

    for step in range(STEPS):
        for f in range(2):
            zx = jnp.zeros((W, ry, LANES), jnp.float32)
            zy = jnp.zeros((rx, W, LANES), jnp.float32)

            @pl.when(me_x == 0)
            def _():
                ext[step, f, 0:W, PADY : PADY + ry, :] = zx

            @pl.when(me_x == n_gx - 1)
            def _():
                ext[step, f, W + rx : 2 * W + rx, PADY : PADY + ry, :] = zx

            @pl.when(me_y == 0)
            def _():
                yrecv[step, f, 0] = zy

            @pl.when(me_y == n_gy - 1)
            def _():
                yrecv[step, f, 1] = zy

    barrier = pltpu.get_barrier_semaphore()
    has = (me_x < n_gx - 1, me_x > 0, me_y < n_gy - 1, me_y > 0)
    up_x = jnp.minimum(me_x + 1, n_gx - 1)
    down_x = jnp.maximum(me_x - 1, 0)
    up_y = jnp.minimum(me_y + 1, n_gy - 1)
    down_y = jnp.maximum(me_y - 1, 0)
    ids = ({"gx": up_x}, {"gx": down_x}, {"gy": up_y}, {"gy": down_y})
    for k in range(4):

        @pl.when(has[k])
        def _():
            pl.semaphore_signal(barrier, inc=1, device_id=ids[k], device_id_type=MESH)

    peers = [lax.rem(me_s + d, n_shot) for d in range(1, n_shot)]
    for peer in peers:
        pl.semaphore_signal(barrier, inc=1, device_id={"shot": peer}, device_id_type=MESH)
    expected = n_shot - 1
    for k in range(4):
        expected = expected + has[k].astype(jnp.int32)

    last_of = ring == RING - 1
    first_of = ring == 0
    crosses = ((last_of & has[0]), (first_of & has[1]))
    relays = ([r for r in range(1, RING)], [r for r in range(RING - 1)])
    straight = (0, RING - 1)
    home = group * RING

    def relay_id(side, r):
        target = home + RING + r if side == 0 else home - RING + r
        return {"gx": jnp.clip(target, 0, n_gx - 1)}

    def is_relay(side, r):
        there = (group > 0) if side == 0 else (group < groups - 1)
        return (ring == r) & there

    def relay_source(side):
        return {"gx": jnp.clip(home - 1 if side == 0 else home + RING, 0, n_gx - 1)}

    def relay_target(side):
        return {"gx": home if side == 0 else home + RING - 1}

    def greet(condition, who):
        @pl.when(condition)
        def _():
            pl.semaphore_signal(barrier, inc=1, device_id=who, device_id_type=MESH)

        return condition.astype(jnp.int32)

    for side in range(2):
        for r in relays[side]:
            expected = expected + greet(crosses[side], relay_id(side, r))
            expected = expected + greet(is_relay(side, r), relay_source(side))
            expected = expected + greet(is_relay(side, r), relay_target(side))
            takes = crosses[1 - side]
            expected = expected + greet(takes, {"gx": home + r})
    pl.semaphore_wait(barrier, expected)

    def x_copy(step, f, side):
        first = (rx - W) if side == 0 else 0
        if step == 0:
            src = fields[f].at[pl.ds(first, W)]
        else:
            src = ext.at[step, f, pl.ds(W + first, W), mid_y]
        dst = ext.at[step, f, pl.ds(0 if side == 0 else W + rx, W), mid_y]
        return pltpu.make_async_remote_copy(
            src_ref=src, dst_ref=dst, send_sem=xs.at[step, f, side, 0], recv_sem=xr.at[step, f, side, 0],
            device_id=ids[side], device_id_type=MESH,
        )

    def y_copy(step, f, side):
        return pltpu.make_async_remote_copy(
            src_ref=ysend.at[step, f, side], dst_ref=yrecv.at[step, f, side],
            send_sem=ys.at[step, f, side], recv_sem=yr.at[step, f, side],
            device_id=ids[2 + side], device_id_type=MESH,
        )

    def piece_copy(step, f, side, piece):
        first = (rx - W) if side == 0 else 0
        if step == 0:
            src = fields[f].at[pl.ds(first + piece, 1)]
        else:
            src = ext.at[step, f, pl.ds(W + first + piece, 1), mid_y]
        if piece == straight[side]:
            dst = ext.at[step, f, pl.ds((0 if side == 0 else W + rx) + piece, 1), mid_y]
            sem, who = xr.at[step, f, side, piece], ids[side]
        else:
            dst = relay.at[step, f, side]
            sem, who = lr.at[step, f, side], relay_id(side, piece)
        return pltpu.make_async_remote_copy(
            src_ref=src, dst_ref=dst, send_sem=xs.at[step, f, side, piece], recv_sem=sem,
            device_id=who, device_id_type=MESH,
        )

    def relay_copy(step, f, side, piece):
        return pltpu.make_async_remote_copy(
            src_ref=relay.at[step, f, side],
            dst_ref=ext.at[step, f, pl.ds((0 if side == 0 else W + rx) + piece, 1), mid_y],
            send_sem=ls.at[step, f, side], recv_sem=xr.at[step, f, side, piece],
            device_id=relay_target(side), device_id_type=MESH,
        )

    def pass_on(step, f):
        for side in range(2):
            for r in relays[side]:

                @pl.when(is_relay(side, r))
                def _():
                    copy = relay_copy(step, f, side, r)
                    pltpu.make_async_remote_copy(
                        src_ref=relay.at[step, f, side], dst_ref=relay.at[step, f, side],
                        send_sem=ls.at[step, f, side], recv_sem=lr.at[step, f, side],
                        device_id=relay_target(side), device_id_type=MESH,
                    ).wait_recv()
                    copy.start()

    def start_x(step, f):
        for side in range(2):

            @pl.when(crosses[side])
            def _():
                for piece in range(W):
                    piece_copy(step, f, side, piece).start()

            @pl.when(has[side] & ~crosses[side])
            def _():
                x_copy(step, f, side).start()

    def start_y(step, f):
        ysend[step, f, 0] = ext[step, f, W : W + rx, PADY + ry - W : PADY + ry, :]
        ysend[step, f, 1] = ext[step, f, W : W + rx, PADY : PADY + W, :]
        for side in range(2):

            @pl.when(has[2 + side])
            def _():
                y_copy(step, f, side).start()

    def wait_x(step, f):
        for side in range(2):

            @pl.when(crosses[1 - side])
            def _():
                for piece in range(W):
                    relay_copy(step, f, side, piece).wait_recv()

            @pl.when(has[1 - side] & ~crosses[1 - side])
            def _():
                x_copy(step, f, side).wait_recv()

    def wait_y(step, f):
        for side in range(2):

            @pl.when(has[3 - side])
            def _():
                y_copy(step, f, side).wait_recv()

        ext[step, f, W : W + rx, PADY - W : PADY, :] = yrecv[step, f, 0]
        ext[step, f, W : W + rx, PADY + ry : PADY + ry + W, :] = yrecv[step, f, 1]

    lane = lax.broadcasted_iota(jnp.int32, (ry, LANES), 1)

    def plane(step, f, x):
        here = ext[step, f, x + W, PADY : PADY + ry, :]
        total = (3.0 * COEFFS[0]) * here
        for k in range(1, W + 1):
            pairs = (
                ext[step, f, x + W + k, PADY : PADY + ry, :] + ext[step, f, x + W - k, PADY : PADY + ry, :]
            ) + (
                ext[step, f, x + W, PADY + k : PADY + ry + k, :]
                + ext[step, f, x + W, PADY - k : PADY + ry - k, :]
            )
            right = jnp.where(lane < LANES - k, pltpu.roll(here, LANES - k, 1), 0.0)
            left = jnp.where(lane >= k, pltpu.roll(here, k, 1), 0.0)
            total = total + COEFFS[k] * (pairs + (right + left))
        return here, total

    def previous(step, f, x):
        if step == 0:
            return last[f, x]
        return ext[step - 1, f, x + W, PADY : PADY + ry, :]

    def advance(step, f, x):
        here, curved = plane(step, f, x)
        if f == 0:
            term = ext[step, 1, x + W, PADY : PADY + ry, :] * curved
            gacc[x] = term if step == 0 else gacc[x] + term
        speed = cour[x]
        fresh = 2.0 * here - previous(step, f, x) + (speed * speed) * curved + adds[f, step, x]
        if step < STEPS - 1:
            ext[step + 1, f, x + W, PADY : PADY + ry, :] = fresh
        else:
            final[f, x] = fresh

    def planes(step, f, low, high):
        def body(x, carry):
            advance(step, f, x)
            return carry

        lax.fori_loop(low, high, body, 0)

    for f in range(2):
        start_x(0, f)
    loads[0].wait()
    start_y(0, 0)
    loads[1].wait()
    start_y(0, 1)
    for copy in loads[2:]:
        copy.wait()
    stores = []
    sends = []
    part_a = (rx - 2 * W) // n_shot
    part_b = 2 * W // n_shot

    def start_a(s):
        return W + s * part_a

    def start_b(s):
        return s * part_b + (s // (n_shot // 2)) * (rx - 2 * W)

    kinds = ((part_a, start_a, rbuf_a), (part_b, start_b, rbuf_b))

    def reduce_start(kind):
        size, start, buf = kinds[kind]
        copies = []
        for d, peer in enumerate(peers):
            copy = pltpu.make_async_remote_copy(
                src_ref=gacc.at[pl.ds(start(peer), size)], dst_ref=buf.at[d],
                send_sem=gs.at[kind, d], recv_sem=gr.at[kind, d],
                device_id={"shot": peer}, device_id_type=MESH,
            )
            copy.start()
            copies.append(copy)
        sends.extend(copies)
        return copies

    def reduce_end(kind, copies):
        size, start, buf = kinds[kind]
        mine = pl.ds(start(me_s), size)
        for copy in copies:
            copy.wait_recv()
        total = gacc[mine]
        for d in range(n_shot - 1):
            total = total + buf[d]
        gout[mine] = total * ((2.0 * GRAD_SCALE) * cour[mine])
        for d, peer in enumerate(peers):
            copy = pltpu.make_async_remote_copy(
                src_ref=gout.at[mine], dst_ref=gout.at[mine],
                send_sem=hs.at[kind, d], recv_sem=hr.at[kind, d],
                device_id={"shot": peer}, device_id_type=MESH,
            )
            copy.start()
            sends.append(copy)

    def gather_wait(kind):
        size, start, buf = kinds[kind]
        for d in range(n_shot - 1):
            other = lax.rem(me_s + n_shot - 1 - d, n_shot)
            theirs = gout.at[pl.ds(start(other), size)]
            pltpu.make_async_remote_copy(
                src_ref=theirs, dst_ref=theirs, send_sem=hs.at[kind, d], recv_sem=hr.at[kind, d],
                device_id={"shot": other}, device_id_type=MESH,
            ).wait_recv()

    end = STEPS - 1
    for step in range(STEPS):
        for f in range(2):
            wait_y(step, f)
            planes(step, f, W, rx - W)
            if step == end and f == 0:
                inner = reduce_start(0)
        for f in range(2):
            pass_on(step, f)
        if step == end:
            reduce_end(0, inner)
        for f in range(2):
            wait_x(step, f)
            planes(step, f, 0, W)
            planes(step, f, rx - W, rx)
            if step < end:
                start_x(step + 1, f)
                start_y(step + 1, f)
            else:
                if f == 0:
                    outer = reduce_start(1)
                copy = pltpu.make_async_copy(final.at[f], (out_p, out_q)[f], store_sem.at[f])
                copy.start()
                stores.append(copy)
    reduce_end(1, outer)
    gather_wait(0)
    gather_wait(1)
    copy = pltpu.make_async_copy(gout, out_g, store_sem.at[2])
    copy.start()
    stores.append(copy)
    for step in range(STEPS):
        for f in range(2):
            for side in range(2):

                @pl.when(crosses[side])
                def _():
                    for piece in range(W):
                        piece_copy(step, f, side, piece).wait_send()

                @pl.when(has[side] & ~crosses[side])
                def _():
                    x_copy(step, f, side).wait_send()

                for r in relays[side]:

                    @pl.when(is_relay(side, r))
                    def _():
                        relay_copy(step, f, side, r).wait_send()

                @pl.when(has[2 + side])
                def _():
                    y_copy(step, f, side).wait_send()

    for copy in sends:
        copy.wait_send()
    for copy in stores:
        copy.wait()


def shards(
    mesh_sizes, forward_now, forward_later, adjoint_now, adjoint_later, courant,
    source_cells, source_wave, receiver_cells, residual,
):
    rx, ry, depth = courant.shape
    n_shot, n_gx, n_gy = mesh_sizes
    f32 = jnp.float32
    chunks = receiver_cells.shape[1] // LANES
    cells = jnp.transpose(receiver_cells, (2, 0, 1)).reshape(3 * chunks, LANES)
    values = residual[0].reshape(STEPS * chunks, LANES)
    scalars = pl.BlockSpec(memory_space=pltpu.SMEM)
    whole = pl.BlockSpec(memory_space=pltpu.VMEM)
    anywhere = pl.BlockSpec(memory_space=pl.ANY)
    block = jax.ShapeDtypeStruct((rx, ry, depth), f32)
    added = jax.ShapeDtypeStruct((STEPS, rx, ry, depth), f32)
    add_p, add_q = pl.pallas_call(
        functools.partial(scatter_kernel, rx, ry, chunks),
        out_shape=(added, added),
        in_specs=[scalars] * 2 + [whole] * 2,
        out_specs=(whole, whole),
        scratch_shapes=[pltpu.VMEM((chunks, LANES), f32), pltpu.VMEM((16 * chunks, LANES), f32)],
        compiler_params=pltpu.CompilerParams(vmem_limit_bytes=WINDOW_LIMIT),
        name="scatter",
    )(source_cells[0], source_wave[0], cells, values)
    sizes = (n_shot, n_gx, n_gy, rx, ry)
    dma = pltpu.SemaphoreType.DMA
    out_p, out_q, out_g = pl.pallas_call(
        functools.partial(wave_kernel, sizes),
        out_shape=(block, block, block),
        in_specs=[anywhere] * 7,
        out_specs=(anywhere,) * 3,
        scratch_shapes=[
            pltpu.VMEM((STEPS, 2, rx + 2 * W, ry + 2 * PADY, depth), f32),
            pltpu.VMEM((2, rx, ry, depth), f32),
            pltpu.VMEM((rx, ry, depth), f32),
            pltpu.VMEM((2, STEPS, rx, ry, depth), f32),
            pltpu.VMEM((2, rx, ry, depth), f32),
            pltpu.VMEM((rx, ry, depth), f32),
            pltpu.VMEM((rx, ry, depth), f32),
            pltpu.VMEM((n_shot - 1, (rx - 2 * W) // n_shot, ry, depth), f32),
            pltpu.VMEM((n_shot - 1, 2 * W // n_shot, ry, depth), f32),
            pltpu.VMEM((STEPS, 2, 2, rx, W, depth), f32),
            pltpu.VMEM((STEPS, 2, 2, rx, W, depth), f32),
            pltpu.VMEM((STEPS, 2, 2, 1, ry, depth), f32),
            dma((7,)),
            dma((STEPS, 2, 2, W)),
            dma((STEPS, 2, 2, W)),
            dma((STEPS, 2, 2)),
            dma((STEPS, 2, 2)),
            dma((2, n_shot - 1)),
            dma((2, n_shot - 1)),
            dma((2, n_shot - 1)),
            dma((2, n_shot - 1)),
            dma((STEPS, 2, 2)),
            dma((STEPS, 2, 2)),
            dma((3,)),
        ],
        compiler_params=pltpu.CompilerParams(
            collective_id=0, has_side_effects=True, vmem_limit_bytes=WINDOW_LIMIT
        ),
        name="window",
    )(
        forward_now[0], forward_later[0], adjoint_now[0], adjoint_later[0], courant, add_p, add_q,
    )
    out_p, out_q, out_g = pl.pallas_call(
        finish_kernel,
        out_shape=(block, block, block),
        in_specs=[anywhere] * 3,
        out_specs=(anywhere,) * 3,
        scratch_shapes=[pltpu.VMEM((3, rx, ry, depth), f32), dma((3,)), dma((3,))],
        compiler_params=pltpu.CompilerParams(vmem_limit_bytes=WINDOW_LIMIT),
        name="finish",
    )(out_p, out_q, out_g)
    return out_p[None], out_q[None], out_g


def solution(mesh):
    field = P("shot", "gx", "gy", None)
    listed = P("shot", None, None)
    sizes = (mesh.shape["shot"], mesh.shape["gx"], mesh.shape["gy"])
    return jax.shard_map(
        functools.partial(shards, sizes),
        mesh=mesh,
        in_specs=(field, field, field, field, P("gx", "gy", None), listed, listed, listed, listed),
        out_specs=(field, field, P("gx", "gy", None)),
        check_vma=False,
    )
```

```python
import functools

import jax
import jax.numpy as jnp
from jax import lax
from jax.experimental import pallas as pl
from jax.experimental.pallas import tpu as pltpu
from jax.sharding import PartitionSpec as P

STEPS = 3
W = 4
PADY = 8
SLOTS = 256
LANES = 128
COEFFS = (-205.0 / 72.0, 8.0 / 5.0, -1.0 / 5.0, 8.0 / 315.0, -1.0 / 560.0)
GRAD_SCALE = 0.1
MESH = pl.DeviceIdType.MESH
WINDOW_LIMIT = 64_000_000
UNROLL = 4


def scatter_kernel(
    rows_x, rows_y, chunks, scells, swave, cells_ref, values_ref, out_p, out_q, rank_ref, feats_ref
):
    cells = rows_x * rows_y
    f32, bf16 = jnp.float32, jnp.bfloat16
    nt = (((1,), (1,)), ((), ()))
    base_x = lax.axis_index("gx") * rows_x
    base_y = lax.axis_index("gy") * rows_y
    out_p[...] = jnp.zeros_like(out_p)
    out_q[...] = jnp.zeros_like(out_q)

    depth_ids = lax.broadcasted_iota(jnp.int32, (1, LANES), 1)

    def one_source(i, carry):
        x = scells[i, 0] - base_x
        y = scells[i, 1] - base_y

        @pl.when((x >= 0) & (x < rows_x) & (y >= 0) & (y < rows_y))
        def _():
            for step in range(STEPS):
                line = out_p[step, x, pl.ds(y, 1), :]
                out_p[step, x, pl.ds(y, 1), :] = line + jnp.where(depth_ids == scells[i, 2], swave[step, i], 0.0)

        return carry

    lax.fori_loop(0, scells.shape[0], one_source, 0)

    x = (cells_ref[0:chunks, :] - base_x).astype(f32)
    y = (cells_ref[chunks : 2 * chunks, :] - base_y).astype(f32)
    inside = (x >= 0.0) & (x < float(rows_x)) & (y >= 0.0) & (y < float(rows_y))
    mask = jnp.where(inside, 1.0, 0.0)
    high = values_ref[...].astype(bf16).astype(f32)
    low = values_ref[...] - high
    parts = [x, y, cells_ref[2 * chunks : 3 * chunks, :].astype(f32)]
    parts += [high[s * chunks : (s + 1) * chunks] for s in range(STEPS)]
    parts += [low[s * chunks : (s + 1) * chunks] for s in range(STEPS)]
    feats_ref[...] = jnp.zeros_like(feats_ref)
    for i, values in enumerate(parts):
        for chunk in range(chunks):
            feats_ref[16 * chunk + i : 16 * chunk + i + 1, :] = values[chunk : chunk + 1, :]
    ones = mask.astype(bf16)
    row = lax.broadcasted_iota(jnp.int32, (LANES, LANES), 0)
    col = lax.broadcasted_iota(jnp.int32, (LANES, LANES), 1)
    upper = (row <= col).astype(f32).astype(bf16)
    inclusive = jnp.dot(ones, upper, preferred_element_type=f32)
    totals = jnp.broadcast_to(inclusive[:, LANES - 1 : LANES], (chunks, LANES)).astype(bf16)
    crow = lax.broadcasted_iota(jnp.int32, (chunks, chunks), 0)
    ccol = lax.broadcasted_iota(jnp.int32, (chunks, chunks), 1)
    before = (ccol < crow).astype(f32).astype(bf16)
    offsets = jnp.dot(before, totals, preferred_element_type=f32)
    rank_ref[...] = jnp.where(inside, offsets + inclusive - 1.0, -1.0)
    count = jnp.sum(mask).astype(jnp.int32)

    def one_round(turn, carry):
        slot = lax.broadcasted_iota(jnp.int32, (SLOTS, LANES), 0).astype(f32)
        base = (turn * SLOTS).astype(f32)
        by_row = jnp.zeros((16, SLOTS), f32)
        by_col = jnp.zeros((SLOTS, 16), f32)
        for chunk in range(chunks):
            rank = rank_ref[chunk : chunk + 1, :] - base
            pick = (slot == rank).astype(f32).astype(bf16)
            part = feats_ref[16 * chunk : 16 * chunk + 16, :].astype(bf16)
            by_row = by_row + lax.dot_general(part, pick, nt, preferred_element_type=f32)
            by_col = by_col + lax.dot_general(pick, part, nt, preferred_element_type=f32)
        place = by_row[0:1, :] * float(rows_y) + by_row[1:2, :]
        ids = lax.broadcasted_iota(jnp.int32, (cells, SLOTS), 0).astype(f32)
        left = (ids == place).astype(f32).astype(bf16)
        lane = lax.broadcasted_iota(jnp.int32, (SLOTS, LANES), 1).astype(f32)
        hit = lane == by_col[:, 2:3]
        for step in range(STEPS):
            upper_part = jnp.where(hit, by_col[:, 3 + step : 4 + step], 0.0)
            lower_part = jnp.where(hit, by_col[:, 6 + step : 7 + step], 0.0)
            right = jnp.concatenate([upper_part, lower_part], axis=1).astype(bf16)
            both = jnp.dot(left, right, preferred_element_type=f32)
            total = (both[:, :LANES] + both[:, LANES:]).reshape(rows_x, rows_y, LANES)
            out_q[step] = out_q[step] + total
        return carry

    lax.fori_loop(0, (count + SLOTS - 1) // SLOTS, one_round, 0)


def finish_kernel(a, b, c, out_a, out_b, out_c, buf, sems_in, sems_out):
    pairs = ((a, out_a), (b, out_b), (c, out_c))
    ins = [pltpu.make_async_copy(src, buf.at[i], sems_in.at[i]) for i, (src, _) in enumerate(pairs)]
    outs = [pltpu.make_async_copy(buf.at[i], dst, sems_out.at[i]) for i, (_, dst) in enumerate(pairs)]
    for copy in ins:
        copy.start()
    for copy_in, copy_out in zip(ins, outs):
        copy_in.wait()
        copy_out.start()
    for copy in outs:
        copy.wait()


def wave_kernel(
    sizes, p0, p2, q0, q2, courant, add_p, add_q, out_p, out_q, out_g,
    ext, last, cour, adds, final, gacc, gout, rbuf_a, rbuf_b, ysend, yrecv,
    load_sem, xs, xr, ys, yr, gs, gr, hs, hr, store_sem,
):
    n_shot, n_gx, n_gy, rx, ry = sizes
    me_s = lax.axis_index("shot")
    me_x = lax.axis_index("gx")
    me_y = lax.axis_index("gy")
    fields = (p0, q0)
    mid_x = pl.ds(W, rx)
    mid_y = pl.ds(PADY, ry)
    loads = []

    def load(src, dst):
        copy = pltpu.make_async_copy(src, dst, load_sem.at[len(loads)])
        copy.start()
        loads.append(copy)

    load(p0, ext.at[0, 0, mid_x, mid_y])
    load(q0, ext.at[0, 1, mid_x, mid_y])
    load(courant, cour)
    load(p2, last.at[0])
    load(q2, last.at[1])
    for step in range(STEPS):
        load(add_p.at[step], adds.at[0, step])
        load(add_q.at[step], adds.at[1, step])

    for step in range(STEPS):
        for f in range(2):
            zx = jnp.zeros((W, ry, LANES), jnp.float32)
            zy = jnp.zeros((rx, W, LANES), jnp.float32)

            @pl.when(me_x == 0)
            def _():
                ext[step, f, 0:W, PADY : PADY + ry, :] = zx

            @pl.when(me_x == n_gx - 1)
            def _():
                ext[step, f, W + rx : 2 * W + rx, PADY : PADY + ry, :] = zx

            @pl.when(me_y == 0)
            def _():
                yrecv[step, f, 0] = zy

            @pl.when(me_y == n_gy - 1)
            def _():
                yrecv[step, f, 1] = zy

    barrier = pltpu.get_barrier_semaphore()
    has = (me_x < n_gx - 1, me_x > 0, me_y < n_gy - 1, me_y > 0)
    up_x = jnp.minimum(me_x + 1, n_gx - 1)
    down_x = jnp.maximum(me_x - 1, 0)
    up_y = jnp.minimum(me_y + 1, n_gy - 1)
    down_y = jnp.maximum(me_y - 1, 0)
    ids = ({"gx": up_x}, {"gx": down_x}, {"gy": up_y}, {"gy": down_y})
    for k in range(4):

        @pl.when(has[k])
        def _():
            pl.semaphore_signal(barrier, inc=1, device_id=ids[k], device_id_type=MESH)

    peers = [lax.rem(me_s + d, n_shot) for d in range(1, n_shot)]
    for peer in peers:
        pl.semaphore_signal(barrier, inc=1, device_id={"shot": peer}, device_id_type=MESH)
    expected = n_shot - 1
    for k in range(4):
        expected = expected + has[k].astype(jnp.int32)

    pl.semaphore_wait(barrier, expected)

    def x_copy(step, f, side):
        first = (rx - W) if side == 0 else 0
        if step == 0:
            src = fields[f].at[pl.ds(first, W)]
        else:
            src = ext.at[step, f, pl.ds(W + first, W), mid_y]
        dst = ext.at[step, f, pl.ds(0 if side == 0 else W + rx, W), mid_y]
        return pltpu.make_async_remote_copy(
            src_ref=src, dst_ref=dst, send_sem=xs.at[step, f, side], recv_sem=xr.at[step, f, side],
            device_id=ids[side], device_id_type=MESH,
        )

    def y_copy(step, f, side):
        return pltpu.make_async_remote_copy(
            src_ref=ysend.at[step, f, side], dst_ref=yrecv.at[step, f, side],
            send_sem=ys.at[step, f, side], recv_sem=yr.at[step, f, side],
            device_id=ids[2 + side], device_id_type=MESH,
        )

    def start_x(step, f):
        for side in range(2):

            @pl.when(has[side])
            def _():
                x_copy(step, f, side).start()

    def start_y(step, f):
        ysend[step, f, 0] = ext[step, f, W : W + rx, PADY + ry - W : PADY + ry, :]
        ysend[step, f, 1] = ext[step, f, W : W + rx, PADY : PADY + W, :]
        for side in range(2):

            @pl.when(has[2 + side])
            def _():
                y_copy(step, f, side).start()

    def wait_x(step, f):
        for side in range(2):

            @pl.when(has[1 - side])
            def _():
                x_copy(step, f, side).wait_recv()

    def wait_y(step, f):
        for side in range(2):

            @pl.when(has[3 - side])
            def _():
                y_copy(step, f, side).wait_recv()

        ext[step, f, W : W + rx, PADY - W : PADY, :] = yrecv[step, f, 0]
        ext[step, f, W : W + rx, PADY + ry : PADY + ry + W, :] = yrecv[step, f, 1]

    lane = lax.broadcasted_iota(jnp.int32, (ry, LANES), 1)

    def plane(step, f, x):
        here = ext[step, f, x + W, PADY : PADY + ry, :]
        total = (3.0 * COEFFS[0]) * here
        for k in range(1, W + 1):
            pairs = (
                ext[step, f, x + W + k, PADY : PADY + ry, :] + ext[step, f, x + W - k, PADY : PADY + ry, :]
            ) + (
                ext[step, f, x + W, PADY + k : PADY + ry + k, :]
                + ext[step, f, x + W, PADY - k : PADY + ry - k, :]
            )
            right = jnp.where(lane < LANES - k, pltpu.roll(here, LANES - k, 1), 0.0)
            left = jnp.where(lane >= k, pltpu.roll(here, k, 1), 0.0)
            total = total + COEFFS[k] * (pairs + (right + left))
        return here, total

    def previous(step, f, x):
        if step == 0:
            return last[f, x]
        return ext[step - 1, f, x + W, PADY : PADY + ry, :]

    def advance(step, f, x):
        here, curved = plane(step, f, x)
        if f == 0:
            term = ext[step, 1, x + W, PADY : PADY + ry, :] * curved
            gacc[x] = term if step == 0 else gacc[x] + term
        speed = cour[x]
        fresh = 2.0 * here - previous(step, f, x) + (speed * speed) * curved + adds[f, step, x]
        if step < STEPS - 1:
            ext[step + 1, f, x + W, PADY : PADY + ry, :] = fresh
        else:
            final[f, x] = fresh

    def planes(step, f, low, high):
        def body(i, carry):
            for k in range(UNROLL):
                advance(step, f, low + i * UNROLL + k)
            return carry

        lax.fori_loop(0, (high - low) // UNROLL, body, 0)

    for f in range(2):
        start_x(0, f)
    loads[0].wait()
    start_y(0, 0)
    loads[1].wait()
    start_y(0, 1)
    for copy in loads[2:5]:
        copy.wait()
    stores = []
    sends = []
    part_a = (rx - 2 * W) // n_shot
    part_b = 2 * W // n_shot

    def start_a(s):
        return W + s * part_a

    def start_b(s):
        return s * part_b + (s // (n_shot // 2)) * (rx - 2 * W)

    kinds = ((part_a, start_a, rbuf_a), (part_b, start_b, rbuf_b))

    def reduce_start(kind):
        size, start, buf = kinds[kind]
        copies = []
        for d, peer in enumerate(peers):
            copy = pltpu.make_async_remote_copy(
                src_ref=gacc.at[pl.ds(start(peer), size)], dst_ref=buf.at[d],
                send_sem=gs.at[kind, d], recv_sem=gr.at[kind, d],
                device_id={"shot": peer}, device_id_type=MESH,
            )
            copy.start()
            copies.append(copy)
        sends.extend(copies)
        return copies

    def reduce_end(kind, copies):
        size, start, buf = kinds[kind]
        mine = pl.ds(start(me_s), size)
        for copy in copies:
            copy.wait_recv()
        total = gacc[mine]
        for d in range(n_shot - 1):
            total = total + buf[d]
        gout[mine] = total * ((2.0 * GRAD_SCALE) * cour[mine])
        for d, peer in enumerate(peers):
            copy = pltpu.make_async_remote_copy(
                src_ref=gout.at[mine], dst_ref=gout.at[mine],
                send_sem=hs.at[kind, d], recv_sem=hr.at[kind, d],
                device_id={"shot": peer}, device_id_type=MESH,
            )
            copy.start()
            sends.append(copy)

    def gather_wait(kind):
        size, start, buf = kinds[kind]
        for d in range(n_shot - 1):
            other = lax.rem(me_s + n_shot - 1 - d, n_shot)
            theirs = gout.at[pl.ds(start(other), size)]
            pltpu.make_async_remote_copy(
                src_ref=theirs, dst_ref=theirs, send_sem=hs.at[kind, d], recv_sem=hr.at[kind, d],
                device_id={"shot": other}, device_id_type=MESH,
            ).wait_recv()

    end = STEPS - 1
    for step in range(STEPS):
        for f in range(2):
            loads[5 + 2 * step + f].wait()
            wait_y(step, f)
            planes(step, f, W, rx - W)
            if step == end and f == 0:
                inner = reduce_start(0)
        if step == end:
            reduce_end(0, inner)
        for f in range(2):
            wait_x(step, f)
            planes(step, f, 0, W)
            planes(step, f, rx - W, rx)
            if step < end:
                start_x(step + 1, f)
                start_y(step + 1, f)
            else:
                if f == 0:
                    outer = reduce_start(1)
                copy = pltpu.make_async_copy(final.at[f], (out_p, out_q)[f], store_sem.at[f])
                copy.start()
                stores.append(copy)
    reduce_end(1, outer)
    gather_wait(0)
    gather_wait(1)
    copy = pltpu.make_async_copy(gout, out_g, store_sem.at[2])
    copy.start()
    stores.append(copy)
    for step in range(STEPS):
        for f in range(2):
            for side in range(2):

                @pl.when(has[side])
                def _():
                    x_copy(step, f, side).wait_send()

                @pl.when(has[2 + side])
                def _():
                    y_copy(step, f, side).wait_send()

    for copy in sends:
        copy.wait_send()
    for copy in stores:
        copy.wait()


def shards(
    mesh_sizes, forward_now, forward_later, adjoint_now, adjoint_later, courant,
    source_cells, source_wave, receiver_cells, residual,
):
    rx, ry, depth = courant.shape
    n_shot, n_gx, n_gy = mesh_sizes
    f32 = jnp.float32
    chunks = receiver_cells.shape[1] // LANES
    cells = jnp.transpose(receiver_cells, (2, 0, 1)).reshape(3 * chunks, LANES)
    values = residual[0].reshape(STEPS * chunks, LANES)
    scalars = pl.BlockSpec(memory_space=pltpu.SMEM)
    whole = pl.BlockSpec(memory_space=pltpu.VMEM)
    anywhere = pl.BlockSpec(memory_space=pl.ANY)
    block = jax.ShapeDtypeStruct((rx, ry, depth), f32)
    added = jax.ShapeDtypeStruct((STEPS, rx, ry, depth), f32)
    add_p, add_q = pl.pallas_call(
        functools.partial(scatter_kernel, rx, ry, chunks),
        out_shape=(added, added),
        in_specs=[scalars] * 2 + [whole] * 2,
        out_specs=(whole, whole),
        scratch_shapes=[pltpu.VMEM((chunks, LANES), f32), pltpu.VMEM((16 * chunks, LANES), f32)],
        compiler_params=pltpu.CompilerParams(vmem_limit_bytes=WINDOW_LIMIT),
        name="scatter",
    )(source_cells[0], source_wave[0], cells, values)
    sizes = (n_shot, n_gx, n_gy, rx, ry)
    dma = pltpu.SemaphoreType.DMA
    out_p, out_q, out_g = pl.pallas_call(
        functools.partial(wave_kernel, sizes),
        out_shape=(block, block, block),
        in_specs=[anywhere] * 7,
        out_specs=(anywhere,) * 3,
        scratch_shapes=[
            pltpu.VMEM((STEPS, 2, rx + 2 * W, ry + 2 * PADY, depth), f32),
            pltpu.VMEM((2, rx, ry, depth), f32),
            pltpu.VMEM((rx, ry, depth), f32),
            pltpu.VMEM((2, STEPS, rx, ry, depth), f32),
            pltpu.VMEM((2, rx, ry, depth), f32),
            pltpu.VMEM((rx, ry, depth), f32),
            pltpu.VMEM((rx, ry, depth), f32),
            pltpu.VMEM((n_shot - 1, (rx - 2 * W) // n_shot, ry, depth), f32),
            pltpu.VMEM((n_shot - 1, 2 * W // n_shot, ry, depth), f32),
            pltpu.VMEM((STEPS, 2, 2, rx, W, depth), f32),
            pltpu.VMEM((STEPS, 2, 2, rx, W, depth), f32),
            dma((5 + 2 * STEPS,)),
            dma((STEPS, 2, 2)),
            dma((STEPS, 2, 2)),
            dma((STEPS, 2, 2)),
            dma((STEPS, 2, 2)),
            dma((2, n_shot - 1)),
            dma((2, n_shot - 1)),
            dma((2, n_shot - 1)),
            dma((2, n_shot - 1)),
            dma((3,)),
        ],
        compiler_params=pltpu.CompilerParams(
            collective_id=0, has_side_effects=True, vmem_limit_bytes=WINDOW_LIMIT
        ),
        name="window",
    )(
        forward_now[0], forward_later[0], adjoint_now[0], adjoint_later[0], courant, add_p, add_q,
    )
    out_p, out_q, out_g = pl.pallas_call(
        finish_kernel,
        out_shape=(block, block, block),
        in_specs=[anywhere] * 3,
        out_specs=(anywhere,) * 3,
        scratch_shapes=[pltpu.VMEM((3, rx, ry, depth), f32), dma((3,)), dma((3,))],
        compiler_params=pltpu.CompilerParams(vmem_limit_bytes=WINDOW_LIMIT),
        name="finish",
    )(out_p, out_q, out_g)
    return out_p[None], out_q[None], out_g


def solution(mesh):
    field = P("shot", "gx", "gy", None)
    listed = P("shot", None, None)
    sizes = (mesh.shape["shot"], mesh.shape["gx"], mesh.shape["gy"])
    return jax.shard_map(
        functools.partial(shards, sizes),
        mesh=mesh,
        in_specs=(field, field, field, field, P("gx", "gy", None), listed, listed, listed, listed),
        out_specs=(field, field, P("gx", "gy", None)),
        check_vma=False,
    )
```

```python
import functools

import jax
import jax.numpy as jnp
from jax import lax
from jax.experimental import pallas as pl
from jax.experimental.pallas import tpu as pltpu
from jax.sharding import PartitionSpec as P

STEPS = 3
W = 4
PADY = 8
SLOTS = 256
LANES = 128
COEFFS = (-205.0 / 72.0, 8.0 / 5.0, -1.0 / 5.0, 8.0 / 315.0, -1.0 / 560.0)
GRAD_SCALE = 0.1
MESH = pl.DeviceIdType.MESH
WINDOW_LIMIT = 64_000_000
UNROLL = 4


def scatter_kernel(
    rows_x, rows_y, chunks, scells, swave, cells_ref, values_ref, out_p, out_q, rank_ref, feats_ref
):
    cells = rows_x * rows_y
    f32, bf16 = jnp.float32, jnp.bfloat16
    nt = (((1,), (1,)), ((), ()))
    base_x = lax.axis_index("gx") * rows_x
    base_y = lax.axis_index("gy") * rows_y
    out_p[...] = jnp.zeros_like(out_p)
    out_q[...] = jnp.zeros_like(out_q)

    depth_ids = lax.broadcasted_iota(jnp.int32, (1, LANES), 1)

    def one_source(i, carry):
        x = scells[0, 0, i] - base_x
        y = scells[1, 0, i] - base_y

        @pl.when((x >= 0) & (x < rows_x) & (y >= 0) & (y < rows_y))
        def _():
            for step in range(STEPS):
                line = out_p[step, x, pl.ds(y, 1), :]
                out_p[step, x, pl.ds(y, 1), :] = line + jnp.where(depth_ids == scells[2, 0, i], swave[step, 0, i], 0.0)

        return carry

    lax.fori_loop(0, scells.shape[2], one_source, 0)

    x = (cells_ref[0:chunks, :] - base_x).astype(f32)
    y = (cells_ref[chunks : 2 * chunks, :] - base_y).astype(f32)
    inside = (x >= 0.0) & (x < float(rows_x)) & (y >= 0.0) & (y < float(rows_y))
    mask = jnp.where(inside, 1.0, 0.0)
    high = values_ref[...].astype(bf16).astype(f32)
    low = values_ref[...] - high
    parts = [x, y, cells_ref[2 * chunks : 3 * chunks, :].astype(f32)]
    parts += [high[s * chunks : (s + 1) * chunks] for s in range(STEPS)]
    parts += [low[s * chunks : (s + 1) * chunks] for s in range(STEPS)]
    feats_ref[...] = jnp.zeros_like(feats_ref)
    for i, values in enumerate(parts):
        for chunk in range(chunks):
            feats_ref[16 * chunk + i : 16 * chunk + i + 1, :] = values[chunk : chunk + 1, :]
    ones = mask.astype(bf16)
    row = lax.broadcasted_iota(jnp.int32, (LANES, LANES), 0)
    col = lax.broadcasted_iota(jnp.int32, (LANES, LANES), 1)
    upper = (row <= col).astype(f32).astype(bf16)
    inclusive = jnp.dot(ones, upper, preferred_element_type=f32)
    totals = jnp.broadcast_to(inclusive[:, LANES - 1 : LANES], (chunks, LANES)).astype(bf16)
    crow = lax.broadcasted_iota(jnp.int32, (chunks, chunks), 0)
    ccol = lax.broadcasted_iota(jnp.int32, (chunks, chunks), 1)
    before = (ccol < crow).astype(f32).astype(bf16)
    offsets = jnp.dot(before, totals, preferred_element_type=f32)
    rank_ref[...] = jnp.where(inside, offsets + inclusive - 1.0, -1.0)
    count = jnp.sum(mask).astype(jnp.int32)

    def one_round(turn, carry):
        slot = lax.broadcasted_iota(jnp.int32, (SLOTS, LANES), 0).astype(f32)
        base = (turn * SLOTS).astype(f32)
        by_row = jnp.zeros((16, SLOTS), f32)
        by_col = jnp.zeros((SLOTS, 16), f32)
        for chunk in range(chunks):
            rank = rank_ref[chunk : chunk + 1, :] - base
            pick = (slot == rank).astype(f32).astype(bf16)
            part = feats_ref[16 * chunk : 16 * chunk + 16, :].astype(bf16)
            by_row = by_row + lax.dot_general(part, pick, nt, preferred_element_type=f32)
            by_col = by_col + lax.dot_general(pick, part, nt, preferred_element_type=f32)
        place = by_row[0:1, :] * float(rows_y) + by_row[1:2, :]
        ids = lax.broadcasted_iota(jnp.int32, (cells, SLOTS), 0).astype(f32)
        left = (ids == place).astype(f32).astype(bf16)
        lane = lax.broadcasted_iota(jnp.int32, (SLOTS, LANES), 1).astype(f32)
        hit = lane == by_col[:, 2:3]
        for step in range(STEPS):
            upper_part = jnp.where(hit, by_col[:, 3 + step : 4 + step], 0.0)
            lower_part = jnp.where(hit, by_col[:, 6 + step : 7 + step], 0.0)
            right = jnp.concatenate([upper_part, lower_part], axis=1).astype(bf16)
            both = jnp.dot(left, right, preferred_element_type=f32)
            total = (both[:, :LANES] + both[:, LANES:]).reshape(rows_x, rows_y, LANES)
            out_q[step] = out_q[step] + total
        return carry

    lax.fori_loop(0, (count + SLOTS - 1) // SLOTS, one_round, 0)


def finish_kernel(a, b, c, out_a, out_b, out_c, buf, sems_in, sems_out):
    pairs = ((a, out_a), (b, out_b), (c, out_c))
    ins = [pltpu.make_async_copy(src, buf.at[i], sems_in.at[i]) for i, (src, _) in enumerate(pairs)]
    outs = [pltpu.make_async_copy(buf.at[i], dst, sems_out.at[i]) for i, (_, dst) in enumerate(pairs)]
    for copy in ins:
        copy.start()
    for copy_in, copy_out in zip(ins, outs):
        copy_in.wait()
        copy_out.start()
    for copy in outs:
        copy.wait()


def wave_kernel(
    sizes, p0, p2, q0, q2, courant, add_p, add_q, out_p, out_q, out_g,
    ext, last, cour, adds, final, gacc, gout, rbuf_a, rbuf_b, ysend, yrecv,
    load_sem, xs, xr, ys, yr, gs, gr, hs, hr, store_sem,
):
    n_shot, n_gx, n_gy, rx, ry = sizes
    me_s = lax.axis_index("shot")
    me_x = lax.axis_index("gx")
    me_y = lax.axis_index("gy")
    fields = (p0, q0)
    mid_x = pl.ds(W, rx)
    mid_y = pl.ds(PADY, ry)
    loads = []

    def load(src, dst):
        copy = pltpu.make_async_copy(src, dst, load_sem.at[len(loads)])
        copy.start()
        loads.append(copy)

    load(p0, ext.at[0, 0, mid_x, mid_y])
    load(q0, ext.at[0, 1, mid_x, mid_y])
    load(courant, cour)
    load(p2, last.at[0])
    load(q2, last.at[1])
    for step in range(STEPS):
        load(add_p.at[step], adds.at[0, step])
        load(add_q.at[step], adds.at[1, step])

    for step in range(STEPS):
        for f in range(2):
            zx = jnp.zeros((W, ry, LANES), jnp.float32)
            zy = jnp.zeros((rx, W, LANES), jnp.float32)

            @pl.when(me_x == 0)
            def _():
                ext[step, f, 0:W, PADY : PADY + ry, :] = zx

            @pl.when(me_x == n_gx - 1)
            def _():
                ext[step, f, W + rx : 2 * W + rx, PADY : PADY + ry, :] = zx

            @pl.when(me_y == 0)
            def _():
                yrecv[step, f, 0] = zy

            @pl.when(me_y == n_gy - 1)
            def _():
                yrecv[step, f, 1] = zy

    barrier = pltpu.get_barrier_semaphore()
    has = (me_x < n_gx - 1, me_x > 0, me_y < n_gy - 1, me_y > 0)
    up_x = jnp.minimum(me_x + 1, n_gx - 1)
    down_x = jnp.maximum(me_x - 1, 0)
    up_y = jnp.minimum(me_y + 1, n_gy - 1)
    down_y = jnp.maximum(me_y - 1, 0)
    ids = ({"gx": up_x}, {"gx": down_x}, {"gy": up_y}, {"gy": down_y})
    for k in range(4):

        @pl.when(has[k])
        def _():
            pl.semaphore_signal(barrier, inc=1, device_id=ids[k], device_id_type=MESH)

    peers = [lax.rem(me_s + d, n_shot) for d in range(1, n_shot)]
    for peer in peers:
        pl.semaphore_signal(barrier, inc=1, device_id={"shot": peer}, device_id_type=MESH)
    expected = n_shot - 1
    for k in range(4):
        expected = expected + has[k].astype(jnp.int32)

    pl.semaphore_wait(barrier, expected)

    def x_copy(step, f, side):
        first = (rx - W) if side == 0 else 0
        if step == 0:
            src = fields[f].at[pl.ds(first, W)]
        else:
            src = ext.at[step, f, pl.ds(W + first, W), mid_y]
        dst = ext.at[step, f, pl.ds(0 if side == 0 else W + rx, W), mid_y]
        return pltpu.make_async_remote_copy(
            src_ref=src, dst_ref=dst, send_sem=xs.at[step, f, side], recv_sem=xr.at[step, f, side],
            device_id=ids[side], device_id_type=MESH,
        )

    def y_copy(step, f, side):
        return pltpu.make_async_remote_copy(
            src_ref=ysend.at[step, f, side], dst_ref=yrecv.at[step, f, side],
            send_sem=ys.at[step, f, side], recv_sem=yr.at[step, f, side],
            device_id=ids[2 + side], device_id_type=MESH,
        )

    def start_x(step, f):
        for side in range(2):

            @pl.when(has[side])
            def _():
                x_copy(step, f, side).start()

    def start_y(step, f):
        ysend[step, f, 0] = ext[step, f, W : W + rx, PADY + ry - W : PADY + ry, :]
        ysend[step, f, 1] = ext[step, f, W : W + rx, PADY : PADY + W, :]
        for side in range(2):

            @pl.when(has[2 + side])
            def _():
                y_copy(step, f, side).start()

    def wait_x(step, f):
        for side in range(2):

            @pl.when(has[1 - side])
            def _():
                x_copy(step, f, side).wait_recv()

    def wait_y(step, f):
        for side in range(2):

            @pl.when(has[3 - side])
            def _():
                y_copy(step, f, side).wait_recv()

        ext[step, f, W : W + rx, PADY - W : PADY, :] = yrecv[step, f, 0]
        ext[step, f, W : W + rx, PADY + ry : PADY + ry + W, :] = yrecv[step, f, 1]

    lane = lax.broadcasted_iota(jnp.int32, (ry, LANES), 1)

    def plane(step, f, x):
        here = ext[step, f, x + W, PADY : PADY + ry, :]
        total = (3.0 * COEFFS[0]) * here
        for k in range(1, W + 1):
            pairs = (
                ext[step, f, x + W + k, PADY : PADY + ry, :] + ext[step, f, x + W - k, PADY : PADY + ry, :]
            ) + (
                ext[step, f, x + W, PADY + k : PADY + ry + k, :]
                + ext[step, f, x + W, PADY - k : PADY + ry - k, :]
            )
            right = jnp.where(lane < LANES - k, pltpu.roll(here, LANES - k, 1), 0.0)
            left = jnp.where(lane >= k, pltpu.roll(here, k, 1), 0.0)
            total = total + COEFFS[k] * (pairs + (right + left))
        return here, total

    def previous(step, f, x):
        if step == 0:
            return last[f, x]
        return ext[step - 1, f, x + W, PADY : PADY + ry, :]

    def advance(step, f, x):
        here, curved = plane(step, f, x)
        if f == 0:
            term = ext[step, 1, x + W, PADY : PADY + ry, :] * curved
            gacc[x] = term if step == 0 else gacc[x] + term
        speed = cour[x]
        fresh = 2.0 * here - previous(step, f, x) + (speed * speed) * curved + adds[f, step, x]
        if step < STEPS - 1:
            ext[step + 1, f, x + W, PADY : PADY + ry, :] = fresh
        else:
            final[f, x] = fresh

    def planes(step, f, low, high):
        def body(i, carry):
            for k in range(UNROLL):
                advance(step, f, low + i * UNROLL + k)
            return carry

        lax.fori_loop(0, (high - low) // UNROLL, body, 0)

    for f in range(2):
        start_x(0, f)
    loads[0].wait()
    start_y(0, 0)
    loads[1].wait()
    start_y(0, 1)
    for copy in loads[2:5]:
        copy.wait()
    stores = []
    sends = []
    part_a = (rx - 2 * W) // n_shot
    part_b = 2 * W // n_shot

    def start_a(s):
        return W + s * part_a

    def start_b(s):
        return s * part_b + (s // (n_shot // 2)) * (rx - 2 * W)

    kinds = ((part_a, start_a, rbuf_a), (part_b, start_b, rbuf_b))

    def reduce_start(kind):
        size, start, buf = kinds[kind]
        copies = []
        for d, peer in enumerate(peers):
            copy = pltpu.make_async_remote_copy(
                src_ref=gacc.at[pl.ds(start(peer), size)], dst_ref=buf.at[d],
                send_sem=gs.at[kind, d], recv_sem=gr.at[kind, d],
                device_id={"shot": peer}, device_id_type=MESH,
            )
            copy.start()
            copies.append(copy)
        sends.extend(copies)
        return copies

    def reduce_end(kind, copies):
        size, start, buf = kinds[kind]
        mine = pl.ds(start(me_s), size)
        for copy in copies:
            copy.wait_recv()
        total = gacc[mine]
        for d in range(n_shot - 1):
            total = total + buf[d]
        gout[mine] = total * ((2.0 * GRAD_SCALE) * cour[mine])
        for d, peer in enumerate(peers):
            copy = pltpu.make_async_remote_copy(
                src_ref=gout.at[mine], dst_ref=gout.at[mine],
                send_sem=hs.at[kind, d], recv_sem=hr.at[kind, d],
                device_id={"shot": peer}, device_id_type=MESH,
            )
            copy.start()
            sends.append(copy)

    def gather_wait(kind):
        size, start, buf = kinds[kind]
        for d in range(n_shot - 1):
            other = lax.rem(me_s + n_shot - 1 - d, n_shot)
            theirs = gout.at[pl.ds(start(other), size)]
            pltpu.make_async_remote_copy(
                src_ref=theirs, dst_ref=theirs, send_sem=hs.at[kind, d], recv_sem=hr.at[kind, d],
                device_id={"shot": other}, device_id_type=MESH,
            ).wait_recv()

    end = STEPS - 1
    for step in range(STEPS):
        for f in range(2):
            loads[5 + 2 * step + f].wait()
            wait_y(step, f)
            planes(step, f, W, rx - W)
            if step == end and f == 0:
                inner = reduce_start(0)
        if step == end:
            reduce_end(0, inner)
        for f in range(2):
            wait_x(step, f)
            planes(step, f, 0, W)
            planes(step, f, rx - W, rx)
            if step < end:
                start_x(step + 1, f)
                start_y(step + 1, f)
            else:
                if f == 0:
                    outer = reduce_start(1)
                copy = pltpu.make_async_copy(final.at[f], (out_p, out_q)[f], store_sem.at[f])
                copy.start()
                stores.append(copy)
    reduce_end(1, outer)
    gather_wait(0)
    gather_wait(1)
    copy = pltpu.make_async_copy(gout, out_g, store_sem.at[2])
    copy.start()
    stores.append(copy)
    for step in range(STEPS):
        for f in range(2):
            for side in range(2):

                @pl.when(has[side])
                def _():
                    x_copy(step, f, side).wait_send()

                @pl.when(has[2 + side])
                def _():
                    y_copy(step, f, side).wait_send()

    for copy in sends:
        copy.wait_send()
    for copy in stores:
        copy.wait()


def shards(
    mesh_sizes, forward_now, forward_later, adjoint_now, adjoint_later, courant,
    source_cells, source_wave, receiver_cells, residual,
):
    rx, ry, depth = courant.shape
    n_shot, n_gx, n_gy = mesh_sizes
    f32 = jnp.float32
    chunks = receiver_cells.shape[1] // LANES
    cells = jnp.transpose(receiver_cells, (2, 0, 1)).reshape(3 * chunks, LANES)
    values = residual[0].reshape(STEPS * chunks, LANES)
    scalars = pl.BlockSpec(memory_space=pltpu.SMEM)
    whole = pl.BlockSpec(memory_space=pltpu.VMEM)
    anywhere = pl.BlockSpec(memory_space=pl.ANY)
    block = jax.ShapeDtypeStruct((rx, ry, depth), f32)
    added = jax.ShapeDtypeStruct((STEPS, rx, ry, depth), f32)
    add_p, add_q = pl.pallas_call(
        functools.partial(scatter_kernel, rx, ry, chunks),
        out_shape=(added, added),
        in_specs=[scalars] * 2 + [whole] * 2,
        out_specs=(whole, whole),
        scratch_shapes=[pltpu.VMEM((chunks, LANES), f32), pltpu.VMEM((16 * chunks, LANES), f32)],
        compiler_params=pltpu.CompilerParams(vmem_limit_bytes=WINDOW_LIMIT),
        name="scatter",
    )(jnp.transpose(source_cells, (2, 0, 1)), jnp.transpose(source_wave, (1, 0, 2)), cells, values)
    sizes = (n_shot, n_gx, n_gy, rx, ry)
    dma = pltpu.SemaphoreType.DMA
    out_p, out_q, out_g = pl.pallas_call(
        functools.partial(wave_kernel, sizes),
        out_shape=(block, block, block),
        in_specs=[anywhere] * 7,
        out_specs=(anywhere,) * 3,
        scratch_shapes=[
            pltpu.VMEM((STEPS, 2, rx + 2 * W, ry + 2 * PADY, depth), f32),
            pltpu.VMEM((2, rx, ry, depth), f32),
            pltpu.VMEM((rx, ry, depth), f32),
            pltpu.VMEM((2, STEPS, rx, ry, depth), f32),
            pltpu.VMEM((2, rx, ry, depth), f32),
            pltpu.VMEM((rx, ry, depth), f32),
            pltpu.VMEM((rx, ry, depth), f32),
            pltpu.VMEM((n_shot - 1, (rx - 2 * W) // n_shot, ry, depth), f32),
            pltpu.VMEM((n_shot - 1, 2 * W // n_shot, ry, depth), f32),
            pltpu.VMEM((STEPS, 2, 2, rx, W, depth), f32),
            pltpu.VMEM((STEPS, 2, 2, rx, W, depth), f32),
            dma((5 + 2 * STEPS,)),
            dma((STEPS, 2, 2)),
            dma((STEPS, 2, 2)),
            dma((STEPS, 2, 2)),
            dma((STEPS, 2, 2)),
            dma((2, n_shot - 1)),
            dma((2, n_shot - 1)),
            dma((2, n_shot - 1)),
            dma((2, n_shot - 1)),
            dma((3,)),
        ],
        compiler_params=pltpu.CompilerParams(
            collective_id=0, has_side_effects=True, vmem_limit_bytes=WINDOW_LIMIT
        ),
        name="window",
    )(
        forward_now[0], forward_later[0], adjoint_now[0], adjoint_later[0], courant, add_p, add_q,
    )
    out_p, out_q, out_g = pl.pallas_call(
        finish_kernel,
        out_shape=(block, block, block),
        in_specs=[anywhere] * 3,
        out_specs=(anywhere,) * 3,
        scratch_shapes=[pltpu.VMEM((3, rx, ry, depth), f32), dma((3,)), dma((3,))],
        compiler_params=pltpu.CompilerParams(vmem_limit_bytes=WINDOW_LIMIT),
        name="finish",
    )(out_p, out_q, out_g)
    return out_p[None], out_q[None], out_g


def solution(mesh):
    field = P("shot", "gx", "gy", None)
    listed = P("shot", None, None)
    sizes = (mesh.shape["shot"], mesh.shape["gx"], mesh.shape["gy"])
    return jax.shard_map(
        functools.partial(shards, sizes),
        mesh=mesh,
        in_specs=(field, field, field, field, P("gx", "gy", None), listed, listed, listed, listed),
        out_specs=(field, field, P("gx", "gy", None)),
        check_vma=False,
    )
```

```python
import functools

import jax
import jax.numpy as jnp
from jax import lax
from jax.experimental import pallas as pl
from jax.experimental.pallas import tpu as pltpu
from jax.sharding import PartitionSpec as P

STEPS = 3
W = 4
PADY = 8
SLOTS = 256
LANES = 128
COEFFS = (-205.0 / 72.0, 8.0 / 5.0, -1.0 / 5.0, 8.0 / 315.0, -1.0 / 560.0)
GRAD_SCALE = 0.1
MESH = pl.DeviceIdType.MESH
WINDOW_LIMIT = 64_000_000
UNROLL = 4


def scatter_kernel(
    rows_x, rows_y, chunks, scells, swave, cells_ref, values_ref, out_p, out_q, rank_ref, feats_ref
):
    cells = rows_x * rows_y
    f32, bf16 = jnp.float32, jnp.bfloat16
    nt = (((1,), (1,)), ((), ()))
    base_x = lax.axis_index("gx") * rows_x
    base_y = lax.axis_index("gy") * rows_y
    out_p[...] = jnp.zeros_like(out_p)
    out_q[...] = jnp.zeros_like(out_q)

    depth_ids = lax.broadcasted_iota(jnp.int32, (1, LANES), 1)

    def one_source(i, carry):
        x = scells[0, 0, i] - base_x
        y = scells[1, 0, i] - base_y

        @pl.when((x >= 0) & (x < rows_x) & (y >= 0) & (y < rows_y))
        def _():
            for step in range(STEPS):
                line = out_p[step, x, pl.ds(y, 1), :]
                out_p[step, x, pl.ds(y, 1), :] = line + jnp.where(depth_ids == scells[2, 0, i], swave[step, 0, i], 0.0)

        return carry

    lax.fori_loop(0, scells.shape[2], one_source, 0)

    x = (cells_ref[0:chunks, :] - base_x).astype(f32)
    y = (cells_ref[chunks : 2 * chunks, :] - base_y).astype(f32)
    inside = (x >= 0.0) & (x < float(rows_x)) & (y >= 0.0) & (y < float(rows_y))
    mask = jnp.where(inside, 1.0, 0.0)
    high = values_ref[...].astype(bf16).astype(f32)
    low = values_ref[...] - high
    parts = [x, y, cells_ref[2 * chunks : 3 * chunks, :].astype(f32)]
    parts += [high[s * chunks : (s + 1) * chunks] for s in range(STEPS)]
    parts += [low[s * chunks : (s + 1) * chunks] for s in range(STEPS)]
    feats_ref[...] = jnp.zeros_like(feats_ref)
    for i, values in enumerate(parts):
        for chunk in range(chunks):
            feats_ref[16 * chunk + i : 16 * chunk + i + 1, :] = values[chunk : chunk + 1, :]
    ones = mask.astype(bf16)
    row = lax.broadcasted_iota(jnp.int32, (LANES, LANES), 0)
    col = lax.broadcasted_iota(jnp.int32, (LANES, LANES), 1)
    upper = (row <= col).astype(f32).astype(bf16)
    inclusive = jnp.dot(ones, upper, preferred_element_type=f32)
    totals = jnp.broadcast_to(inclusive[:, LANES - 1 : LANES], (chunks, LANES)).astype(bf16)
    crow = lax.broadcasted_iota(jnp.int32, (chunks, chunks), 0)
    ccol = lax.broadcasted_iota(jnp.int32, (chunks, chunks), 1)
    before = (ccol < crow).astype(f32).astype(bf16)
    offsets = jnp.dot(before, totals, preferred_element_type=f32)
    rank_ref[...] = jnp.where(inside, offsets + inclusive - 1.0, -1.0)
    count = jnp.sum(mask).astype(jnp.int32)

    def one_round(turn, carry):
        slot = lax.broadcasted_iota(jnp.int32, (SLOTS, LANES), 0).astype(f32)
        base = (turn * SLOTS).astype(f32)
        by_row = jnp.zeros((16, SLOTS), f32)
        by_col = jnp.zeros((SLOTS, 16), f32)
        for chunk in range(chunks):
            rank = rank_ref[chunk : chunk + 1, :] - base
            pick = (slot == rank).astype(f32).astype(bf16)
            part = feats_ref[16 * chunk : 16 * chunk + 16, :].astype(bf16)
            by_row = by_row + lax.dot_general(part, pick, nt, preferred_element_type=f32)
            by_col = by_col + lax.dot_general(pick, part, nt, preferred_element_type=f32)
        place = by_row[0:1, :] * float(rows_y) + by_row[1:2, :]
        ids = lax.broadcasted_iota(jnp.int32, (cells, SLOTS), 0).astype(f32)
        left = (ids == place).astype(f32).astype(bf16)
        lane = lax.broadcasted_iota(jnp.int32, (SLOTS, LANES), 1).astype(f32)
        hit = lane == by_col[:, 2:3]
        for step in range(STEPS):
            upper_part = jnp.where(hit, by_col[:, 3 + step : 4 + step], 0.0)
            lower_part = jnp.where(hit, by_col[:, 6 + step : 7 + step], 0.0)
            right = jnp.concatenate([upper_part, lower_part], axis=1).astype(bf16)
            both = jnp.dot(left, right, preferred_element_type=f32)
            total = (both[:, :LANES] + both[:, LANES:]).reshape(rows_x, rows_y, LANES)
            out_q[step] = out_q[step] + total
        return carry

    lax.fori_loop(0, (count + SLOTS - 1) // SLOTS, one_round, 0)


def finish_kernel(a, b, c, out_a, out_b, out_c, buf, sems_in, sems_out):
    pairs = ((a, out_a), (b, out_b), (c, out_c))
    ins = [pltpu.make_async_copy(src, buf.at[i], sems_in.at[i]) for i, (src, _) in enumerate(pairs)]
    outs = [pltpu.make_async_copy(buf.at[i], dst, sems_out.at[i]) for i, (_, dst) in enumerate(pairs)]
    for copy in ins:
        copy.start()
    for copy_in, copy_out in zip(ins, outs):
        copy_in.wait()
        copy_out.start()
    for copy in outs:
        copy.wait()


def wave_kernel(
    sizes, p0, p2, q0, q2, courant, add_p, add_q, out_p, out_q, out_g,
    ext, last, cour, adds, final, gacc, gout, rbuf_a, rbuf_b, ysend, yrecv,
    load_sem, xs, xr, ys, yr, gs, gr, hs, hr, store_sem,
):
    n_shot, n_gx, n_gy, rx, ry = sizes
    me_s = lax.axis_index("shot")
    me_x = lax.axis_index("gx")
    me_y = lax.axis_index("gy")
    fields = (p0, q0)
    mid_x = pl.ds(W, rx)
    mid_y = pl.ds(PADY, ry)
    loads = []

    def load(src, dst):
        copy = pltpu.make_async_copy(src, dst, load_sem.at[len(loads)])
        copy.start()
        loads.append(copy)

    load(p0, ext.at[0, 0, mid_x, mid_y])
    load(q0, ext.at[0, 1, mid_x, mid_y])
    load(courant, cour)
    load(p2, last.at[0])
    load(q2, last.at[1])
    for step in range(STEPS):
        load(add_p.at[step], adds.at[0, step])
        load(add_q.at[step], adds.at[1, step])

    for step in range(STEPS):
        for f in range(2):
            zx = jnp.zeros((W, ry, LANES), jnp.float32)
            zy = jnp.zeros((rx, W, LANES), jnp.float32)

            @pl.when(me_x == 0)
            def _():
                ext[step, f, 0:W, PADY : PADY + ry, :] = zx

            @pl.when(me_x == n_gx - 1)
            def _():
                ext[step, f, W + rx : 2 * W + rx, PADY : PADY + ry, :] = zx

            @pl.when(me_y == 0)
            def _():
                yrecv[step, f, 0] = zy

            @pl.when(me_y == n_gy - 1)
            def _():
                yrecv[step, f, 1] = zy

    barrier = pltpu.get_barrier_semaphore()
    has = (me_x < n_gx - 1, me_x > 0, me_y < n_gy - 1, me_y > 0)
    up_x = jnp.minimum(me_x + 1, n_gx - 1)
    down_x = jnp.maximum(me_x - 1, 0)
    up_y = jnp.minimum(me_y + 1, n_gy - 1)
    down_y = jnp.maximum(me_y - 1, 0)
    ids = ({"gx": up_x}, {"gx": down_x}, {"gy": up_y}, {"gy": down_y})
    for k in range(4):

        @pl.when(has[k])
        def _():
            pl.semaphore_signal(barrier, inc=1, device_id=ids[k], device_id_type=MESH)

    peers = [lax.rem(me_s + d, n_shot) for d in range(1, n_shot)]
    for peer in peers:
        pl.semaphore_signal(barrier, inc=1, device_id={"shot": peer}, device_id_type=MESH)
    expected = n_shot - 1
    for k in range(4):
        expected = expected + has[k].astype(jnp.int32)

    pl.semaphore_wait(barrier, expected)

    def x_copy(step, f, side):
        first = (rx - W) if side == 0 else 0
        if step == 0:
            src = fields[f].at[pl.ds(first, W)]
        else:
            src = ext.at[step, f, pl.ds(W + first, W), mid_y]
        dst = ext.at[step, f, pl.ds(0 if side == 0 else W + rx, W), mid_y]
        return pltpu.make_async_remote_copy(
            src_ref=src, dst_ref=dst, send_sem=xs.at[step, f, side], recv_sem=xr.at[step, f, side],
            device_id=ids[side], device_id_type=MESH,
        )

    def y_copy(step, f, side):
        return pltpu.make_async_remote_copy(
            src_ref=ysend.at[step, f, side], dst_ref=yrecv.at[step, f, side],
            send_sem=ys.at[step, f, side], recv_sem=yr.at[step, f, side],
            device_id=ids[2 + side], device_id_type=MESH,
        )

    def start_x(step, f):
        for side in range(2):

            @pl.when(has[side])
            def _():
                x_copy(step, f, side).start()

    def start_y(step, f):
        ysend[step, f, 0] = ext[step, f, W : W + rx, PADY + ry - W : PADY + ry, :]
        ysend[step, f, 1] = ext[step, f, W : W + rx, PADY : PADY + W, :]
        for side in range(2):

            @pl.when(has[2 + side])
            def _():
                y_copy(step, f, side).start()

    def wait_x(step, f):
        for side in range(2):

            @pl.when(has[1 - side])
            def _():
                x_copy(step, f, side).wait_recv()

    def wait_y(step, f):
        for side in range(2):

            @pl.when(has[3 - side])
            def _():
                y_copy(step, f, side).wait_recv()

        ext[step, f, W : W + rx, PADY - W : PADY, :] = yrecv[step, f, 0]
        ext[step, f, W : W + rx, PADY + ry : PADY + ry + W, :] = yrecv[step, f, 1]

    lane = lax.broadcasted_iota(jnp.int32, (ry, LANES), 1)

    def plane(step, f, x):
        here = ext[step, f, x + W, PADY : PADY + ry, :]
        total = (3.0 * COEFFS[0]) * here
        for k in range(1, W + 1):
            pairs = (
                ext[step, f, x + W + k, PADY : PADY + ry, :] + ext[step, f, x + W - k, PADY : PADY + ry, :]
            ) + (
                ext[step, f, x + W, PADY + k : PADY + ry + k, :]
                + ext[step, f, x + W, PADY - k : PADY + ry - k, :]
            )
            right = jnp.where(lane < LANES - k, pltpu.roll(here, LANES - k, 1), 0.0)
            left = jnp.where(lane >= k, pltpu.roll(here, k, 1), 0.0)
            total = total + COEFFS[k] * (pairs + (right + left))
        return here, total

    def previous(step, f, x):
        if step == 0:
            return last[f, x]
        return ext[step - 1, f, x + W, PADY : PADY + ry, :]

    def advance(step, f, x):
        here, curved = plane(step, f, x)
        if f == 0:
            term = ext[step, 1, x + W, PADY : PADY + ry, :] * curved
            gacc[x] = term if step == 0 else gacc[x] + term
        speed = cour[x]
        fresh = 2.0 * here - previous(step, f, x) + (speed * speed) * curved + adds[f, step, x]
        if step < STEPS - 1:
            ext[step + 1, f, x + W, PADY : PADY + ry, :] = fresh
        else:
            final[f, x] = fresh

    def planes(step, f, low, high):
        turn = 2 * UNROLL if (high - low) % (2 * UNROLL) == 0 else UNROLL

        def body(i, carry):
            for k in range(turn):
                advance(step, f, low + i * turn + k)
            return carry

        lax.fori_loop(0, (high - low) // turn, body, 0)

    for f in range(2):
        start_x(0, f)
    loads[0].wait()
    start_y(0, 0)
    loads[1].wait()
    start_y(0, 1)
    for copy in loads[2:5]:
        copy.wait()
    stores = []
    sends = []
    part_a = (rx - 2 * W) // n_shot
    part_b = 2 * W // n_shot

    def start_a(s):
        return W + s * part_a

    def start_b(s):
        return s * part_b + (s // (n_shot // 2)) * (rx - 2 * W)

    kinds = ((part_a, start_a, rbuf_a), (part_b, start_b, rbuf_b))

    def reduce_start(kind):
        size, start, buf = kinds[kind]
        copies = []
        for d, peer in enumerate(peers):
            copy = pltpu.make_async_remote_copy(
                src_ref=gacc.at[pl.ds(start(peer), size)], dst_ref=buf.at[d],
                send_sem=gs.at[kind, d], recv_sem=gr.at[kind, d],
                device_id={"shot": peer}, device_id_type=MESH,
            )
            copy.start()
            copies.append(copy)
        sends.extend(copies)
        return copies

    def reduce_end(kind, copies):
        size, start, buf = kinds[kind]
        mine = pl.ds(start(me_s), size)
        for copy in copies:
            copy.wait_recv()
        total = gacc[mine]
        for d in range(n_shot - 1):
            total = total + buf[d]
        gout[mine] = total * ((2.0 * GRAD_SCALE) * cour[mine])
        for d, peer in enumerate(peers):
            copy = pltpu.make_async_remote_copy(
                src_ref=gout.at[mine], dst_ref=gout.at[mine],
                send_sem=hs.at[kind, d], recv_sem=hr.at[kind, d],
                device_id={"shot": peer}, device_id_type=MESH,
            )
            copy.start()
            sends.append(copy)

    def gather_wait(kind):
        size, start, buf = kinds[kind]
        for d in range(n_shot - 1):
            other = lax.rem(me_s + n_shot - 1 - d, n_shot)
            theirs = gout.at[pl.ds(start(other), size)]
            pltpu.make_async_remote_copy(
                src_ref=theirs, dst_ref=theirs, send_sem=hs.at[kind, d], recv_sem=hr.at[kind, d],
                device_id={"shot": other}, device_id_type=MESH,
            ).wait_recv()

    end = STEPS - 1
    for step in range(STEPS):
        for f in range(2):
            loads[5 + 2 * step + f].wait()
            wait_y(step, f)
            planes(step, f, W, rx - W)
            if step == end and f == 0:
                inner = reduce_start(0)
        if step == end:
            reduce_end(0, inner)
        for f in range(2):
            wait_x(step, f)
            planes(step, f, 0, W)
            planes(step, f, rx - W, rx)
            if step < end:
                start_x(step + 1, f)
                start_y(step + 1, f)
            else:
                if f == 0:
                    outer = reduce_start(1)
                copy = pltpu.make_async_copy(final.at[f], (out_p, out_q)[f], store_sem.at[f])
                copy.start()
                stores.append(copy)
    reduce_end(1, outer)
    gather_wait(0)
    gather_wait(1)
    copy = pltpu.make_async_copy(gout, out_g, store_sem.at[2])
    copy.start()
    stores.append(copy)
    for step in range(STEPS):
        for f in range(2):
            for side in range(2):

                @pl.when(has[side])
                def _():
                    x_copy(step, f, side).wait_send()

                @pl.when(has[2 + side])
                def _():
                    y_copy(step, f, side).wait_send()

    for copy in sends:
        copy.wait_send()
    for copy in stores:
        copy.wait()


def shards(
    mesh_sizes, forward_now, forward_later, adjoint_now, adjoint_later, courant,
    source_cells, source_wave, receiver_cells, residual,
):
    rx, ry, depth = courant.shape
    n_shot, n_gx, n_gy = mesh_sizes
    f32 = jnp.float32
    chunks = receiver_cells.shape[1] // LANES
    cells = jnp.transpose(receiver_cells, (2, 0, 1)).reshape(3 * chunks, LANES)
    values = residual[0].reshape(STEPS * chunks, LANES)
    scalars = pl.BlockSpec(memory_space=pltpu.SMEM)
    whole = pl.BlockSpec(memory_space=pltpu.VMEM)
    anywhere = pl.BlockSpec(memory_space=pl.ANY)
    block = jax.ShapeDtypeStruct((rx, ry, depth), f32)
    added = jax.ShapeDtypeStruct((STEPS, rx, ry, depth), f32)
    add_p, add_q = pl.pallas_call(
        functools.partial(scatter_kernel, rx, ry, chunks),
        out_shape=(added, added),
        in_specs=[scalars] * 2 + [whole] * 2,
        out_specs=(whole, whole),
        scratch_shapes=[pltpu.VMEM((chunks, LANES), f32), pltpu.VMEM((16 * chunks, LANES), f32)],
        compiler_params=pltpu.CompilerParams(vmem_limit_bytes=WINDOW_LIMIT),
        name="scatter",
    )(jnp.transpose(source_cells, (2, 0, 1)), jnp.transpose(source_wave, (1, 0, 2)), cells, values)
    sizes = (n_shot, n_gx, n_gy, rx, ry)
    dma = pltpu.SemaphoreType.DMA
    out_p, out_q, out_g = pl.pallas_call(
        functools.partial(wave_kernel, sizes),
        out_shape=(block, block, block),
        in_specs=[anywhere] * 7,
        out_specs=(anywhere,) * 3,
        scratch_shapes=[
            pltpu.VMEM((STEPS, 2, rx + 2 * W, ry + 2 * PADY, depth), f32),
            pltpu.VMEM((2, rx, ry, depth), f32),
            pltpu.VMEM((rx, ry, depth), f32),
            pltpu.VMEM((2, STEPS, rx, ry, depth), f32),
            pltpu.VMEM((2, rx, ry, depth), f32),
            pltpu.VMEM((rx, ry, depth), f32),
            pltpu.VMEM((rx, ry, depth), f32),
            pltpu.VMEM((n_shot - 1, (rx - 2 * W) // n_shot, ry, depth), f32),
            pltpu.VMEM((n_shot - 1, 2 * W // n_shot, ry, depth), f32),
            pltpu.VMEM((STEPS, 2, 2, rx, W, depth), f32),
            pltpu.VMEM((STEPS, 2, 2, rx, W, depth), f32),
            dma((5 + 2 * STEPS,)),
            dma((STEPS, 2, 2)),
            dma((STEPS, 2, 2)),
            dma((STEPS, 2, 2)),
            dma((STEPS, 2, 2)),
            dma((2, n_shot - 1)),
            dma((2, n_shot - 1)),
            dma((2, n_shot - 1)),
            dma((2, n_shot - 1)),
            dma((3,)),
        ],
        compiler_params=pltpu.CompilerParams(
            collective_id=0, has_side_effects=True, vmem_limit_bytes=WINDOW_LIMIT
        ),
        name="window",
    )(
        forward_now[0], forward_later[0], adjoint_now[0], adjoint_later[0], courant, add_p, add_q,
    )
    out_p, out_q, out_g = pl.pallas_call(
        finish_kernel,
        out_shape=(block, block, block),
        in_specs=[anywhere] * 3,
        out_specs=(anywhere,) * 3,
        scratch_shapes=[pltpu.VMEM((3, rx, ry, depth), f32), dma((3,)), dma((3,))],
        compiler_params=pltpu.CompilerParams(vmem_limit_bytes=WINDOW_LIMIT),
        name="finish",
    )(out_p, out_q, out_g)
    return out_p[None], out_q[None], out_g


def solution(mesh):
    field = P("shot", "gx", "gy", None)
    listed = P("shot", None, None)
    sizes = (mesh.shape["shot"], mesh.shape["gx"], mesh.shape["gy"])
    return jax.shard_map(
        functools.partial(shards, sizes),
        mesh=mesh,
        in_specs=(field, field, field, field, P("gx", "gy", None), listed, listed, listed, listed),
        out_specs=(field, field, P("gx", "gy", None)),
        check_vma=False,
    )
```
